256 devices in a mesh: pipe: 16 (over y, x), expert: 16 (over z, core).
Axes of the slice: x: 4, y: 4, z: 8, core: 2. Of those that a mesh axis runs over, the one named last changes fastest.
Arguments:
- streams: bfloat16 [16, 2, 1024, 3584], P('pipe', None, 'expert'), may hold values from -6 to 6
- norm_gain: float32 [16, 3584], P('pipe'), may hold values from 0.25 to 1.75
- w_gate: bfloat16 [16, 16, 3584, 512], P('pipe', 'expert'), may hold values from -0.09375 to 0.09375
- w_up: bfloat16 [16, 16, 3584, 512], P('pipe', 'expert'), may hold values from -0.09375 to 0.09375
- w_down: bfloat16 [16, 16, 512, 3584], P('pipe', 'expert'), may hold values from -0.1875 to 0.1875
- routes: int32 [16, 2, 1024, 2], P('pipe', None, 'expert'), may hold values from 0 to 7, all different within a row; in each aligned block of 64 rows (0 to 63, 64 to 127, ..., all dimensions but the last counted through in order) at most 32 rows name the same one
- gate_weights: float32 [16, 2, 1024, 2], P('pipe', None, 'expert'), may hold values from 0.2 to 1.2
Outputs:
- next_streams: bfloat16 [16, 2, 1024, 3584], P('pipe', None, 'expert')
The draws below stay inside these ranges and needn't reach their ends.
Inputs may be any that keep to these rules, and one draw needn't show every extreme that they name: `routes`: each token names 2 different experts. Within each aligned block of 64 tokens of a micro-batch (the tokens of one device of the expert axis), at most 32 tokens name the same expert, a bound that some block reaches.
All inputs are finite; a program needn't handle non-finite values.
Results may differ from the reference program's by a relative error of at most 0.0051.
Values may be sent and summed in bfloat16 or wider, within the bound.
A program may use at most 128 MiB of HBM per device.

```python
import math
import jax
import jax.numpy as jnp
import numpy as np
from jax import lax

D = 3584
FF = 1024
TOPK = 2
TOK_DEV = 64
EXPERTS = 8
TOKENS = 1024
CAP = 32
N_PIPE = 16
N_EXPERT = 16


def block_levels(key, extent, split, smallest, high):
    def one(position, shards_of):
        draws = jax.random.uniform(jax.random.fold_in(jax.random.fold_in(key, 6), position), (shards_of,), jnp.float32, smallest / len(split), high / len(split))
        return jnp.repeat(jnp.exp(draws), extent[position] // shards_of).reshape((-1,) + (1,) * (len(extent) - position - 1))

    level = one(*split[0])
    for cut in split[1:]:
        level = level * one(*cut)
    return level


def assign_block(key, own, number, rows, number_of, top, bound, skew):
    order = jax.random.permutation(key, number_of)
    packed, ordinary = load_shares(number_of, rows * top, bound, skew, True), load_shares(number_of, rows * top, bound, skew, False)
    places = jnp.arange(number_of)

    def named(sizes, offset_by):
        used = int((sizes > 0).sum())
        fixed = max(1, used // 4)
        moved = fixed + (places - fixed + offset_by * (used - fixed)) % max(1, number_of - fixed)
        return jnp.zeros((number_of,), jnp.int32).at[order[jnp.where(places < fixed, places, moved)]].set(jnp.asarray(sizes, jnp.int32))

    sizes = jnp.where(number % 4 == 0, named(packed, number // 4), named(ordinary, number - number // 4 - 1))
    mixed = jax.random.permutation(jax.random.fold_in(own, 3), number_of)
    giver, sink = mixed[0:number_of // 2 * 2:2], mixed[1:number_of // 2 * 2:2]
    room = jnp.minimum(sizes[giver] - 1, bound - sizes[sink]) // 2
    room = jnp.where((giver == order[0]) | (sink == order[0]) | (sizes[sink] == 0), 0, jnp.maximum(room, 0))
    moved = jax.random.randint(jax.random.fold_in(own, 4), (number_of // 2,), 0, 1 << 20) % (room + 1)
    sizes = sizes.at[giver].add(-moved).at[sink].add(moved)
    members = jnp.searchsorted(jnp.cumsum(sizes), jnp.arange(rows * top), side="right").astype(jnp.int32)
    grid = members.reshape(top, rows).T
    grid = grid[jax.random.permutation(jax.random.fold_in(own, 1), rows)]
    offset_by = jax.random.randint(jax.random.fold_in(own, 2), (rows, 1), 0, top)
    return jnp.take_along_axis(grid, (jnp.arange(top)[None, :] + offset_by) % top, axis=1)


def load_shares(number_of, total, limit, slope, full):
    weights = [(1 << 20) // math.isqrt(standing ** slope) + 1 for standing in range(1, number_of + 1)]
    largest = limit if full else min(limit, max(-(-total // number_of), total * weights[0] // sum(weights)))
    least = 1 if total - largest >= number_of - 1 else 0
    given, rest = [largest] + [least] * (number_of - 1), total - largest - least * (number_of - 1)
    while rest > 0:
        movable = [i for i in range(1, number_of) if given[i] < largest] or [i for i in range(1, number_of) if given[i] < limit]
        pool, remaining = sum([weights[i] for i in movable]), rest
        for i in movable:
            extra = min(limit - given[i], max(1, remaining * weights[i] // pool), rest)
            given[i] = given[i] + extra
            rest = rest - extra
    return np.array(given)


def noise(own_key, extent, scale, most, cuts=(), held_as=jnp.bfloat16):
    level = block_levels(own_key, extent, cuts, -0.22, 0.18) if cuts else 1.0
    drawn = jax.random.normal(own_key, extent, jnp.float32) * scale * level
    return jnp.minimum(jnp.maximum(drawn, -most), most).astype(held_as)


def setup_inputs(seed: int = 0) -> dict:
    keys = jax.random.split(jax.random.key(seed), 8)
    streams = noise(keys[0], (N_PIPE, 2, TOKENS, D), 1.0, 6.0, ((0, 16), (2, 16)))
    norm_gain = jnp.clip(1.0 + 0.15 * jax.random.normal(keys[1], (N_PIPE, D), jnp.float32), 0.25, 1.75)
    w_gate = noise(keys[2], (N_PIPE, 2 * EXPERTS, D, FF // 2), D ** -0.5, 0.09375, ((0, 16), (1, 16)))
    w_up = noise(keys[3], (N_PIPE, 2 * EXPERTS, D, FF // 2), D ** -0.5, 0.09375, ((0, 16), (1, 16)))
    w_down = noise(keys[4], (N_PIPE, 2 * EXPERTS, FF // 2, D), FF ** -0.5, 0.1875, ((0, 16), (1, 16)))
    routes_keys = jax.random.split(jax.random.fold_in(keys[5], 1), N_PIPE * 2 * TOKENS // TOK_DEV)
    routes_turns = jax.random.permutation(jax.random.fold_in(keys[5], 3), N_PIPE * 2 * TOKENS // TOK_DEV)
    routes = jax.vmap(lambda own, number: assign_block(jax.random.fold_in(keys[5], 2), own, number, TOK_DEV, EXPERTS, TOPK, CAP, 2))(routes_keys, routes_turns).reshape((N_PIPE, 2, TOKENS, TOPK))
    gate_weights = jnp.clip(0.2 + 1 * jax.random.uniform(keys[6], (N_PIPE, 2, TOKENS, TOPK), jnp.float32) ** block_levels(keys[6], (N_PIPE, 2, TOKENS, TOPK), ((0, 16), (2, 16)), -0.2, 0.2), 0.2, 1.2)
    return dict(streams=streams, norm_gain=norm_gain, w_gate=w_gate, w_up=w_up, w_down=w_down, routes=routes, gate_weights=gate_weights)


def section_layer(operands):
    state_in, gain_row, gate_shard, up_shard, down_shard, chosen_all, weight_all = operands
    gate_full = gate_shard.reshape(EXPERTS, 2, D, FF // 2).transpose(0, 2, 1, 3).reshape(EXPERTS, D, FF)
    up_full = up_shard.reshape(EXPERTS, 2, D, FF // 2).transpose(0, 2, 1, 3).reshape(EXPERTS, D, FF)
    down_pair = down_shard.reshape(EXPERTS, 2, FF // 2, D)
    outputs = []
    for stream in range(2):
        state = state_in[stream].astype(jnp.float32)
        normed = (state * lax.rsqrt(lax.optimization_barrier(jnp.mean(state * state, axis=-1, keepdims=True)) + 1e-06) * gain_row).astype(jnp.bfloat16)
        blocks = chosen_all[stream].reshape(N_EXPERT, TOK_DEV * TOPK)
        onehot = (blocks[:, :, None] == jnp.arange(EXPERTS, dtype=jnp.int32)[None, None, :]).astype(jnp.int32)
        slot_rank = lax.optimization_barrier(jnp.sum((jnp.cumsum(onehot, axis=1) - onehot) * onehot, axis=-1)).astype(jnp.int32)
        column = (jnp.arange(N_EXPERT, dtype=jnp.int32)[:, None] * CAP + slot_rank).astype(jnp.int32)
        token_index = jnp.broadcast_to(jnp.arange(TOKENS, dtype=jnp.int32).reshape(N_EXPERT, TOK_DEV)[:, :, None], (N_EXPERT, TOK_DEV, TOPK)).reshape(N_EXPERT, TOK_DEV * TOPK)
        table = jnp.zeros((EXPERTS, N_EXPERT * CAP), jnp.int32).at[blocks, column].set(token_index)

        def one_expert(pieces):
            rows_of, gate_mat, up_mat, down_mats = pieces
            row_block = normed[rows_of]
            gate_val = jnp.dot(row_block, gate_mat, preferred_element_type=jnp.float32)
            up_val = jnp.dot(row_block, up_mat, preferred_element_type=jnp.float32)
            hidden = (jax.nn.silu(gate_val) * up_val).astype(jnp.bfloat16)
            first = jnp.dot(hidden[:, :FF // 2], down_mats[0], preferred_element_type=jnp.float32).astype(jnp.bfloat16)
            second = jnp.dot(hidden[:, FF // 2:], down_mats[1], preferred_element_type=jnp.float32).astype(jnp.bfloat16)
            return first.astype(jnp.float32) + second.astype(jnp.float32)
        expert_rows = lax.map(one_expert, (table, gate_full, up_full, down_pair))
        picked = expert_rows[blocks.reshape(-1), column.reshape(-1)].reshape(TOKENS, TOPK, D)
        mixed = state + lax.optimization_barrier(jnp.sum(weight_all[stream][:, :, None] * picked, axis=1))
        outputs.append(mixed.astype(jnp.bfloat16))
    return jnp.stack(outputs)

def reference(streams, norm_gain, w_gate, w_up, w_down, routes, gate_weights):
    layer_out = lax.map(section_layer, (streams, norm_gain, w_gate, w_up, w_down, routes, gate_weights))
    upward = jnp.roll(layer_out[:, 0], 1, axis=0)
    downward = jnp.roll(layer_out[:, 1], -1, axis=0)
    return jnp.stack([upward, downward], axis=1)
```

```python
import jax
import jax.numpy as jnp
import numpy as np
from jax import lax
from jax.sharding import Mesh
from jax.sharding import PartitionSpec as P


def from_behind(value, axis, steps):
    count = lax.axis_size(axis)
    pairs = [(source, (source + steps) % count) for source in range(count)]
    return lax.ppermute(value, axis, pairs)


def shard_ffn(row_block, gate_local, up_local, down_local):
    gate_val = jnp.dot(row_block, gate_local, preferred_element_type=jnp.float32)
    up_val = jnp.dot(row_block, up_local, preferred_element_type=jnp.float32)
    hidden = (jax.nn.silu(gate_val) * up_val).astype(jnp.bfloat16)
    return jnp.dot(hidden, down_local, preferred_element_type=jnp.float32).astype(jnp.bfloat16)


def expert_pass(outgoing, gate_local, up_local, down_local):
    chips, capacity, width = outgoing.shape
    arrived = lax.all_to_all(outgoing, "ez", split_axis=0, concat_axis=0, tiled=True)
    sibling_rows = from_behind(arrived, "ec", 1)
    rows = chips * capacity
    theirs = shard_ffn(sibling_rows.reshape(rows, width), gate_local, up_local, down_local)
    returned_half = from_behind(theirs, "ec", 1)
    mine = shard_ffn(arrived.reshape(rows, width), gate_local, up_local, down_local)
    summed = (mine.astype(jnp.float32) + returned_half.astype(jnp.float32)).astype(jnp.bfloat16)
    back = lax.all_to_all(
        summed.reshape(chips, capacity, width), "ez", split_axis=0, concat_axis=0, tiled=True
    )
    return back.astype(jnp.float32)


def body(streams, norm_gain, w_gate, w_up, w_down, routes, gate_weights):
    experts = lax.axis_size("ez")
    gate_local = w_gate[0, 0]
    up_local = w_up[0, 0]
    down_local = w_down[0, 0]
    gain_row = norm_gain[0]
    tok_rows = streams.shape[2]
    width = streams.shape[3]
    top_count = routes.shape[3]
    capacity = 2 * tok_rows * top_count // experts
    lane_count = experts * capacity
    lane_index = jnp.arange(lane_count, dtype=jnp.int32)
    expert_index = jnp.arange(experts, dtype=jnp.int32)
    results = []
    for stream in range(2):
        state = streams[0, stream].astype(jnp.float32)
        normed = (
            state * lax.rsqrt(jnp.mean(state * state, axis=-1, keepdims=True) + 1e-06) * gain_row
        ).astype(jnp.bfloat16)
        chosen = routes[0, stream].reshape(-1)
        onehot = (chosen[:, None] == expert_index[None, :]).astype(jnp.int32)
        slot_rank = jnp.sum((jnp.cumsum(onehot, axis=0) - onehot) * onehot, axis=1)
        lane_of = chosen * capacity + slot_rank
        matches = lane_index[:, None] == lane_of[None, :]
        send_matrix = jnp.sum(
            matches.reshape(lane_count, tok_rows, top_count).astype(jnp.float32), axis=-1
        ).astype(jnp.bfloat16)
        outgoing = jnp.dot(send_matrix, normed, preferred_element_type=jnp.float32).astype(
            jnp.bfloat16
        )
        outgoing = outgoing.reshape(experts, capacity, width)
        weights = gate_weights[0, stream].reshape(-1)
        combine = jnp.sum(
            (matches.astype(jnp.float32) * weights[None, :]).reshape(
                lane_count, tok_rows, top_count
            ),
            axis=-1,
        ).T
        expert_rows = expert_pass(outgoing, gate_local, up_local, down_local)
        mixed = state + jnp.dot(
            combine,
            expert_rows.reshape(lane_count, width),
            precision=lax.Precision.HIGHEST,
            preferred_element_type=jnp.float32,
        )
        results.append(mixed.astype(jnp.bfloat16))
    forward = from_behind(results[0], "pipe", 1)
    backward = from_behind(results[1], "pipe", -1)
    return jnp.stack([forward, backward])[None]


def solution(mesh):
    pipe_size, expert_size = mesh.devices.shape
    split = Mesh(
        np.asarray(mesh.devices).reshape(pipe_size, expert_size // 2, 2), ("pipe", "ez", "ec")
    )
    tok = ("ez", "ec")
    return jax.shard_map(
        body,
        mesh=split,
        in_specs=(
            P("pipe", None, tok, None),
            P("pipe", None),
            P("pipe", tok, None, None),
            P("pipe", tok, None, None),
            P("pipe", tok, None, None),
            P("pipe", None, tok, None),
            P("pipe", None, tok, None),
        ),
        out_specs=P("pipe", None, tok, None),
        check_vma=False,
    )
```

```python
import jax
import jax.numpy as jnp
import numpy as np
from jax import lax
from jax.sharding import Mesh
from jax.sharding import PartitionSpec as P


def from_behind(value, axis, steps):
    count = lax.axis_size(axis)
    pairs = [(source, (source + steps) % count) for source in range(count)]
    return lax.ppermute(value, axis, pairs)


def full_ffn(row_block, gate_full, up_full, down_pair):
    gate_val = jnp.dot(row_block, gate_full, preferred_element_type=jnp.float32)
    up_val = jnp.dot(row_block, up_full, preferred_element_type=jnp.float32)
    hidden = (jax.nn.silu(gate_val) * up_val).astype(jnp.bfloat16)
    half = down_pair.shape[1]
    first = jnp.dot(hidden[:, :half], down_pair[0], preferred_element_type=jnp.float32)
    second = jnp.dot(hidden[:, half:], down_pair[1], preferred_element_type=jnp.float32)
    summed = first.astype(jnp.bfloat16).astype(jnp.float32) + second.astype(
        jnp.bfloat16
    ).astype(jnp.float32)
    return summed.astype(jnp.bfloat16)


def expert_pass(outgoing, gate_full, up_full, down_pair):
    chips, capacity, width = outgoing.shape
    arrived = lax.all_to_all(outgoing, "ez", split_axis=0, concat_axis=0, tiled=True)
    summed = full_ffn(arrived.reshape(chips * capacity, width), gate_full, up_full, down_pair)
    back = lax.all_to_all(
        summed.reshape(chips, capacity, width), "ez", split_axis=0, concat_axis=0, tiled=True
    )
    return back.astype(jnp.float32)


def body(streams, norm_gain, w_gate, w_up, w_down, routes, gate_weights):
    experts = lax.axis_size("ez")
    gate_full = jnp.concatenate(lax.all_gather(w_gate[0, 0], "ec"), axis=1)
    up_full = jnp.concatenate(lax.all_gather(w_up[0, 0], "ec"), axis=1)
    down_pair = lax.all_gather(w_down[0, 0], "ec")
    gain_row = norm_gain[0]
    tok_rows = streams.shape[2]
    width = streams.shape[3]
    top_count = routes.shape[3]
    capacity = 2 * tok_rows * top_count // experts
    lane_count = experts * capacity
    lane_index = jnp.arange(lane_count, dtype=jnp.int32)
    expert_index = jnp.arange(experts, dtype=jnp.int32)
    results = []
    for stream in range(2):
        state = streams[0, stream].astype(jnp.float32)
        normed = (
            state * lax.rsqrt(jnp.mean(state * state, axis=-1, keepdims=True) + 1e-06) * gain_row
        ).astype(jnp.bfloat16)
        chosen = routes[0, stream].reshape(-1)
        onehot = (chosen[:, None] == expert_index[None, :]).astype(jnp.int32)
        slot_rank = jnp.sum((jnp.cumsum(onehot, axis=0) - onehot) * onehot, axis=1)
        lane_of = chosen * capacity + slot_rank
        matches = lane_index[:, None] == lane_of[None, :]
        send_matrix = jnp.sum(
            matches.reshape(lane_count, tok_rows, top_count).astype(jnp.float32), axis=-1
        ).astype(jnp.bfloat16)
        outgoing = jnp.dot(send_matrix, normed, preferred_element_type=jnp.float32).astype(
            jnp.bfloat16
        )
        outgoing = outgoing.reshape(experts, capacity, width)
        weights = gate_weights[0, stream].reshape(-1)
        combine = jnp.sum(
            (matches.astype(jnp.float32) * weights[None, :]).reshape(
                lane_count, tok_rows, top_count
            ),
            axis=-1,
        ).T
        expert_rows = expert_pass(outgoing, gate_full, up_full, down_pair)
        mixed = state + jnp.dot(
            combine,
            expert_rows.reshape(lane_count, width),
            precision=lax.Precision.HIGHEST,
            preferred_element_type=jnp.float32,
        )
        results.append(mixed.astype(jnp.bfloat16))
    forward = from_behind(results[0], "pipe", 1)
    backward = from_behind(results[1], "pipe", -1)
    return jnp.stack([forward, backward])[None]


def solution(mesh):
    pipe_size, expert_size = mesh.devices.shape
    split = Mesh(
        np.asarray(mesh.devices).reshape(pipe_size, expert_size // 2, 2), ("pipe", "ez", "ec")
    )
    tok = ("ez", "ec")
    return jax.shard_map(
        body,
        mesh=split,
        in_specs=(
            P("pipe", None, tok, None),
            P("pipe", None),
            P("pipe", tok, None, None),
            P("pipe", tok, None, None),
            P("pipe", tok, None, None),
            P("pipe", None, tok, None),
            P("pipe", None, tok, None),
        ),
        out_specs=P("pipe", None, tok, None),
        check_vma=False,
    )
```

```python
import functools

import jax
import jax.numpy as jnp
import numpy as np
from jax import lax
from jax.experimental import pallas as pl
from jax.experimental.pallas import tpu as pltpu
from jax.sharding import Mesh
from jax.sharding import PartitionSpec as P


def from_behind(value, axis, steps):
    count = lax.axis_size(axis)
    pairs = [(source, (source + steps) % count) for source in range(count)]
    return lax.ppermute(value, axis, pairs)


MESH = pl.DeviceIdType.MESH


def moe_kernel(
    chips, xs_hbm, wg_hbm, wu_hbm, wd_hbm, ys_hbm,
    recv, res, wg, wu, wd, dsend, drecv, rsend, rrecv, lsem, wsem,
):
    streams, rows, width = recv.shape
    cap = rows // chips
    pipe = lax.axis_index("pipe")
    me = lax.axis_index("ez")
    core = lax.axis_index("ec")

    def dev(p):
        return (pipe, p, core)

    def blk(p):
        return pl.ds(pl.multiple_of(p * cap, cap), cap)

    weight_copies = [
        pltpu.make_async_copy(wg_hbm, wg, wsem.at[0]),
        pltpu.make_async_copy(wu_hbm, wu, wsem.at[1]),
        pltpu.make_async_copy(wd_hbm, wd, wsem.at[2]),
    ]
    for c in weight_copies:
        c.start()

    barrier = pltpu.get_barrier_semaphore()
    for k in range(1, chips):
        pl.semaphore_signal(
            barrier, inc=1, device_id=dev(lax.rem(me + k, chips)), device_id_type=MESH
        )
    pl.semaphore_wait(barrier, chips - 1)

    def dispatch(s, k):
        p = lax.rem(me + k, chips)
        return pltpu.make_async_remote_copy(
            src_ref=xs_hbm.at[s, blk(p)], dst_ref=recv.at[s, blk(me)],
            send_sem=dsend.at[s, k], recv_sem=drecv.at[s, me],
            device_id=dev(p), device_id_type=MESH,
        )

    def dispatch_in(s, k):
        q = lax.rem(me + chips - k, chips)
        return pltpu.make_async_remote_copy(
            src_ref=xs_hbm.at[s, blk(q)], dst_ref=recv.at[s, blk(q)],
            send_sem=dsend.at[s, k], recv_sem=drecv.at[s, q],
            device_id=dev(q), device_id_type=MESH,
        )

    def back(s, k):
        p = lax.rem(me + k, chips)
        return pltpu.make_async_remote_copy(
            src_ref=res.at[s, blk(p)], dst_ref=ys_hbm.at[s, blk(me)],
            send_sem=rsend.at[s, k], recv_sem=rrecv.at[s, me],
            device_id=dev(p), device_id_type=MESH,
        )

    def back_in(s, k):
        q = lax.rem(me + chips - k, chips)
        return pltpu.make_async_remote_copy(
            src_ref=res.at[s, blk(q)], dst_ref=ys_hbm.at[s, blk(q)],
            send_sem=rsend.at[s, k], recv_sem=rrecv.at[s, q],
            device_id=dev(q), device_id_type=MESH,
        )

    local_in = [
        pltpu.make_async_copy(xs_hbm.at[s, blk(me)], recv.at[s, blk(me)], lsem.at[0, s])
        for s in range(streams)
    ]
    local_out = [
        pltpu.make_async_copy(res.at[s, blk(me)], ys_hbm.at[s, blk(me)], lsem.at[1, s])
        for s in range(streams)
    ]
    for s in range(streams):
        local_in[s].start()
        for k in range(1, chips):
            dispatch(s, k).start()
    for c in weight_copies:
        c.wait()

    tile = 128
    for s in range(streams):
        local_in[s].wait()
        for k in range(1, chips):
            dispatch_in(s, k).wait_recv()
        for b in range(rows // tile):
            x = recv[s, pl.ds(b * tile, tile), :]
            total = None
            for j in range(2):
                gate_val = jnp.dot(x, wg[j], preferred_element_type=jnp.float32)
                up_val = jnp.dot(x, wu[j], preferred_element_type=jnp.float32)
                hidden = (jax.nn.silu(gate_val) * up_val).astype(jnp.bfloat16)
                part = jnp.dot(hidden, wd[j], preferred_element_type=jnp.float32)
                part = part.astype(jnp.bfloat16).astype(jnp.float32)
                total = part if total is None else total + part
            res[s, pl.ds(b * tile, tile), :] = total.astype(jnp.bfloat16)
        local_out[s].start()
        for k in range(1, chips):
            back(s, k).start()

    for s in range(streams):
        for k in range(1, chips):
            dispatch(s, k).wait_send()
    for s in range(streams):
        local_out[s].wait()
        for k in range(1, chips):
            back(s, k).wait_send()
        for k in range(1, chips):
            back_in(s, k).wait_recv()


def expert_pass(outgoing, gate_pair, up_pair, down_pair):
    streams, rows, width = outgoing.shape
    chips = lax.axis_size("ez")
    hbm = pl.BlockSpec(memory_space=pl.ANY)
    return pl.pallas_call(
        functools.partial(moe_kernel, chips),
        out_shape=jax.ShapeDtypeStruct(outgoing.shape, jnp.bfloat16),
        in_specs=[hbm] * 4,
        out_specs=hbm,
        scratch_shapes=[
            pltpu.VMEM(outgoing.shape, jnp.bfloat16),
            pltpu.VMEM(outgoing.shape, jnp.bfloat16),
            pltpu.VMEM(gate_pair.shape, jnp.bfloat16),
            pltpu.VMEM(up_pair.shape, jnp.bfloat16),
            pltpu.VMEM(down_pair.shape, jnp.bfloat16),
            pltpu.SemaphoreType.DMA((streams, chips)),
            pltpu.SemaphoreType.DMA((streams, chips)),
            pltpu.SemaphoreType.DMA((streams, chips)),
            pltpu.SemaphoreType.DMA((streams, chips)),
            pltpu.SemaphoreType.DMA((2, streams)),
            pltpu.SemaphoreType.DMA((3,)),
        ],
        compiler_params=pltpu.CompilerParams(
            collective_id=0, has_side_effects=True, vmem_limit_bytes=62 * 1024 * 1024
        ),
    )(outgoing, gate_pair, up_pair, down_pair)


def body(streams, norm_gain, w_gate, w_up, w_down, routes, gate_weights):
    experts = lax.axis_size("ez")
    gate_pair = lax.all_gather(w_gate[0, 0], "ec")
    up_pair = lax.all_gather(w_up[0, 0], "ec")
    down_pair = lax.all_gather(w_down[0, 0], "ec")
    gain_row = norm_gain[0]
    tok_rows = streams.shape[2]
    width = streams.shape[3]
    top_count = routes.shape[3]
    capacity = 2 * tok_rows * top_count // experts
    lane_count = experts * capacity
    lane_index = jnp.arange(lane_count, dtype=jnp.int32)
    expert_index = jnp.arange(experts, dtype=jnp.int32)
    states, outgoings, combines = [], [], []
    for stream in range(2):
        state = streams[0, stream].astype(jnp.float32)
        normed = (
            state * lax.rsqrt(jnp.mean(state * state, axis=-1, keepdims=True) + 1e-06) * gain_row
        ).astype(jnp.bfloat16)
        chosen = routes[0, stream].reshape(-1)
        onehot = (chosen[:, None] == expert_index[None, :]).astype(jnp.int32)
        slot_rank = jnp.sum((jnp.cumsum(onehot, axis=0) - onehot) * onehot, axis=1)
        lane_of = chosen * capacity + slot_rank
        matches = lane_index[:, None] == lane_of[None, :]
        send_matrix = jnp.sum(
            matches.reshape(lane_count, tok_rows, top_count).astype(jnp.float32), axis=-1
        ).astype(jnp.bfloat16)
        outgoing = jnp.dot(send_matrix, normed, preferred_element_type=jnp.float32).astype(
            jnp.bfloat16
        )
        weights = gate_weights[0, stream].reshape(-1)
        combine = jnp.sum(
            (matches.astype(jnp.float32) * weights[None, :]).reshape(
                lane_count, tok_rows, top_count
            ),
            axis=-1,
        ).T
        states.append(state)
        outgoings.append(outgoing)
        combines.append(combine)
    expert_rows = expert_pass(jnp.stack(outgoings), gate_pair, up_pair, down_pair)
    results = []
    for stream in range(2):
        mixed = states[stream] + jnp.dot(
            combines[stream],
            expert_rows[stream].astype(jnp.float32),
            precision=lax.Precision.HIGHEST,
            preferred_element_type=jnp.float32,
        )
        results.append(mixed.astype(jnp.bfloat16))
    forward = from_behind(results[0], "pipe", 1)
    backward = from_behind(results[1], "pipe", -1)
    return jnp.stack([forward, backward])[None]


def solution(mesh):
    pipe_size, expert_size = mesh.devices.shape
    split = Mesh(
        np.asarray(mesh.devices).reshape(pipe_size, expert_size // 2, 2), ("pipe", "ez", "ec")
    )
    tok = ("ez", "ec")
    return jax.shard_map(
        body,
        mesh=split,
        in_specs=(
            P("pipe", None, tok, None),
            P("pipe", None),
            P("pipe", tok, None, None),
            P("pipe", tok, None, None),
            P("pipe", tok, None, None),
            P("pipe", None, tok, None),
            P("pipe", None, tok, None),
        ),
        out_specs=P("pipe", None, tok, None),
        check_vma=False,
    )
```

```python
import functools

import jax
import jax.numpy as jnp
import numpy as np
from jax import lax
from jax.experimental import pallas as pl
from jax.experimental.pallas import tpu as pltpu
from jax.sharding import Mesh
from jax.sharding import PartitionSpec as P


def from_behind(value, axis, steps):
    count = lax.axis_size(axis)
    pairs = [(source, (source + steps) % count) for source in range(count)]
    return lax.ppermute(value, axis, pairs)


MESH = pl.DeviceIdType.MESH


def moe_kernel(
    chips, xs_hbm, wg_hbm, wu_hbm, wd_hbm, ys_hbm,
    recv, res, wg, wu, wd, dsend, drecv, rsend, rrecv, lsem, wsem,
):
    streams, rows, width = recv.shape
    cap = rows // chips
    pipe = lax.axis_index("pipe")
    me = lax.axis_index("ez")
    core = lax.axis_index("ec")

    def dev(p):
        return (pipe, p, core)

    def blk(p):
        return pl.ds(pl.multiple_of(p * cap, cap), cap)

    sibling = (pipe, me, 1 - core)
    weights = ((wg_hbm, wg), (wu_hbm, wu), (wd_hbm, wd))
    own_copies = [
        pltpu.make_async_copy(src, dst.at[core], wsem.at[0, i])
        for i, (src, dst) in enumerate(weights)
    ]
    for c in own_copies:
        c.start()

    barrier = pltpu.get_barrier_semaphore()
    for k in range(1, chips):
        pl.semaphore_signal(
            barrier, inc=1, device_id=dev(lax.rem(me + k, chips)), device_id_type=MESH
        )
    pl.semaphore_signal(barrier, inc=1, device_id=sibling, device_id_type=MESH)
    pl.semaphore_wait(barrier, chips)

    to_sibling = [
        pltpu.make_async_remote_copy(
            src_ref=src, dst_ref=dst.at[core], send_sem=wsem.at[1, i], recv_sem=wsem.at[2, i],
            device_id=sibling, device_id_type=MESH,
        )
        for i, (src, dst) in enumerate(weights)
    ]
    from_sibling = [
        pltpu.make_async_remote_copy(
            src_ref=src, dst_ref=dst.at[1 - core], send_sem=wsem.at[1, i],
            recv_sem=wsem.at[2, i], device_id=sibling, device_id_type=MESH,
        )
        for i, (src, dst) in enumerate(weights)
    ]

    def dispatch(s, k):
        p = lax.rem(me + k, chips)
        return pltpu.make_async_remote_copy(
            src_ref=xs_hbm.at[s, blk(p)], dst_ref=recv.at[s, blk(me)],
            send_sem=dsend.at[s, k], recv_sem=drecv.at[s, me],
            device_id=dev(p), device_id_type=MESH,
        )

    def dispatch_in(s, k):
        q = lax.rem(me + chips - k, chips)
        return pltpu.make_async_remote_copy(
            src_ref=xs_hbm.at[s, blk(q)], dst_ref=recv.at[s, blk(q)],
            send_sem=dsend.at[s, k], recv_sem=drecv.at[s, q],
            device_id=dev(q), device_id_type=MESH,
        )

    def back(s, k):
        p = lax.rem(me + k, chips)
        return pltpu.make_async_remote_copy(
            src_ref=res.at[s, blk(p)], dst_ref=ys_hbm.at[s, blk(me)],
            send_sem=rsend.at[s, k], recv_sem=rrecv.at[s, me],
            device_id=dev(p), device_id_type=MESH,
        )

    def back_in(s, k):
        q = lax.rem(me + chips - k, chips)
        return pltpu.make_async_remote_copy(
            src_ref=res.at[s, blk(q)], dst_ref=ys_hbm.at[s, blk(q)],
            send_sem=rsend.at[s, k], recv_sem=rrecv.at[s, q],
            device_id=dev(q), device_id_type=MESH,
        )

    local_in = [
        pltpu.make_async_copy(xs_hbm.at[s, blk(me)], recv.at[s, blk(me)], lsem.at[0, s])
        for s in range(streams)
    ]
    local_out = [
        pltpu.make_async_copy(res.at[s, blk(me)], ys_hbm.at[s, blk(me)], lsem.at[1, s])
        for s in range(streams)
    ]
    for s in range(streams):
        local_in[s].start()
        for k in range(1, chips):
            dispatch(s, k).start()
    for c in to_sibling:
        c.start()
    for c in own_copies:
        c.wait()
    for c in from_sibling:
        c.wait_recv()
    for c in to_sibling:
        c.wait_send()

    tile = 128
    for s in range(streams):
        local_in[s].wait()
        for k in range(1, chips):
            dispatch_in(s, k).wait_recv()
        for b in range(rows // tile):
            x = recv[s, pl.ds(b * tile, tile), :]
            total = None
            for j in range(2):
                gate_val = jnp.dot(x, wg[j], preferred_element_type=jnp.float32)
                up_val = jnp.dot(x, wu[j], preferred_element_type=jnp.float32)
                hidden = (jax.nn.silu(gate_val) * up_val).astype(jnp.bfloat16)
                part = jnp.dot(hidden, wd[j], preferred_element_type=jnp.float32)
                part = part.astype(jnp.bfloat16).astype(jnp.float32)
                total = part if total is None else total + part
            res[s, pl.ds(b * tile, tile), :] = total.astype(jnp.bfloat16)
        local_out[s].start()
        for k in range(1, chips):
            back(s, k).start()

    for s in range(streams):
        for k in range(1, chips):
            dispatch(s, k).wait_send()
    for s in range(streams):
        local_out[s].wait()
        for k in range(1, chips):
            back(s, k).wait_send()
        for k in range(1, chips):
            back_in(s, k).wait_recv()


def expert_pass(outgoing, gate_half, up_half, down_half):
    streams, rows, width = outgoing.shape
    chips = lax.axis_size("ez")
    hbm = pl.BlockSpec(memory_space=pl.ANY)
    return pl.pallas_call(
        functools.partial(moe_kernel, chips),
        out_shape=jax.ShapeDtypeStruct(outgoing.shape, jnp.bfloat16),
        in_specs=[hbm] * 4,
        out_specs=hbm,
        scratch_shapes=[
            pltpu.VMEM(outgoing.shape, jnp.bfloat16),
            pltpu.VMEM(outgoing.shape, jnp.bfloat16),
            pltpu.VMEM((2,) + gate_half.shape, jnp.bfloat16),
            pltpu.VMEM((2,) + up_half.shape, jnp.bfloat16),
            pltpu.VMEM((2,) + down_half.shape, jnp.bfloat16),
            pltpu.SemaphoreType.DMA((streams, chips)),
            pltpu.SemaphoreType.DMA((streams, chips)),
            pltpu.SemaphoreType.DMA((streams, chips)),
            pltpu.SemaphoreType.DMA((streams, chips)),
            pltpu.SemaphoreType.DMA((2, streams)),
            pltpu.SemaphoreType.DMA((3, 3)),
        ],
        compiler_params=pltpu.CompilerParams(
            collective_id=0, has_side_effects=True, vmem_limit_bytes=62 * 1024 * 1024
        ),
    )(outgoing, gate_half, up_half, down_half)


def body(streams, norm_gain, w_gate, w_up, w_down, routes, gate_weights):
    experts = lax.axis_size("ez")
    gain_row = norm_gain[0]
    tok_rows = streams.shape[2]
    width = streams.shape[3]
    top_count = routes.shape[3]
    capacity = 2 * tok_rows * top_count // experts
    lane_count = experts * capacity
    lane_index = jnp.arange(lane_count, dtype=jnp.int32)
    expert_index = jnp.arange(experts, dtype=jnp.int32)
    states, outgoings, combines = [], [], []
    for stream in range(2):
        state = streams[0, stream].astype(jnp.float32)
        normed = (
            state * lax.rsqrt(jnp.mean(state * state, axis=-1, keepdims=True) + 1e-06) * gain_row
        ).astype(jnp.bfloat16)
        chosen = routes[0, stream].reshape(-1)
        onehot = (chosen[:, None] == expert_index[None, :]).astype(jnp.int32)
        slot_rank = jnp.sum((jnp.cumsum(onehot, axis=0) - onehot) * onehot, axis=1)
        lane_of = chosen * capacity + slot_rank
        matches = lane_index[:, None] == lane_of[None, :]
        send_matrix = jnp.sum(
            matches.reshape(lane_count, tok_rows, top_count).astype(jnp.float32), axis=-1
        ).astype(jnp.bfloat16)
        outgoing = jnp.dot(send_matrix, normed, preferred_element_type=jnp.float32).astype(
            jnp.bfloat16
        )
        weights = gate_weights[0, stream].reshape(-1)
        combine = jnp.sum(
            (matches.astype(jnp.float32) * weights[None, :]).reshape(
                lane_count, tok_rows, top_count
            ),
            axis=-1,
        ).T
        states.append(state)
        outgoings.append(outgoing)
        combines.append(combine)
    expert_rows = expert_pass(jnp.stack(outgoings), w_gate[0, 0], w_up[0, 0], w_down[0, 0])
    results = []
    for stream in range(2):
        mixed = states[stream] + jnp.dot(
            combines[stream],
            expert_rows[stream].astype(jnp.float32),
            precision=lax.Precision.HIGHEST,
            preferred_element_type=jnp.float32,
        )
        results.append(mixed.astype(jnp.bfloat16))
    forward = from_behind(results[0], "pipe", 1)
    backward = from_behind(results[1], "pipe", -1)
    return jnp.stack([forward, backward])[None]


def solution(mesh):
    pipe_size, expert_size = mesh.devices.shape
    split = Mesh(
        np.asarray(mesh.devices).reshape(pipe_size, expert_size // 2, 2), ("pipe", "ez", "ec")
    )
    tok = ("ez", "ec")
    return jax.shard_map(
        body,
        mesh=split,
        in_specs=(
            P("pipe", None, tok, None),
            P("pipe", None),
            P("pipe", tok, None, None),
            P("pipe", tok, None, None),
            P("pipe", tok, None, None),
            P("pipe", None, tok, None),
            P("pipe", None, tok, None),
        ),
        out_specs=P("pipe", None, tok, None),
        check_vma=False,
    )
```

```python
import functools

import jax
import jax.numpy as jnp
import numpy as np
from jax import lax
from jax.experimental import pallas as pl
from jax.experimental.pallas import tpu as pltpu
from jax.sharding import Mesh
from jax.sharding import PartitionSpec as P


def from_behind(value, axis, steps):
    count = lax.axis_size(axis)
    pairs = [(source, (source + steps) % count) for source in range(count)]
    return lax.ppermute(value, axis, pairs)


MESH = pl.DeviceIdType.MESH


def moe_kernel(
    chips, xs_hbm, wg_hbm, wu_hbm, wd_hbm, state_ref, hi_ref, lo_ref, next_hbm,
    recv, res, ys, mixed, wg, wu, wd, dsend, drecv, rsend, rrecv, lsem, wsem, psem,
):
    streams, rows, width = recv.shape
    cap = rows // chips
    pipe = lax.axis_index("pipe")
    pipes = lax.axis_size("pipe")
    me = lax.axis_index("ez")
    core = lax.axis_index("ec")

    def dev(p):
        return (pipe, p, core)

    def blk(p):
        return pl.ds(pl.multiple_of(p * cap, cap), cap)

    sibling = (pipe, me, 1 - core)
    weights = ((wg_hbm, wg), (wu_hbm, wu), (wd_hbm, wd))
    own_copies = [
        pltpu.make_async_copy(src, dst.at[core], wsem.at[0, i])
        for i, (src, dst) in enumerate(weights)
    ]
    for c in own_copies:
        c.start()

    barrier = pltpu.get_barrier_semaphore()
    for k in range(1, chips):
        pl.semaphore_signal(
            barrier, inc=1, device_id=dev(lax.rem(me + k, chips)), device_id_type=MESH
        )
    pl.semaphore_signal(barrier, inc=1, device_id=sibling, device_id_type=MESH)
    section = (lax.rem(pipe + 1, pipes), lax.rem(pipe + pipes - 1, pipes))
    for p in section:
        pl.semaphore_signal(barrier, inc=1, device_id=(p, me, core), device_id_type=MESH)
    pl.semaphore_wait(barrier, chips + 2)

    to_sibling = [
        pltpu.make_async_remote_copy(
            src_ref=src, dst_ref=dst.at[core], send_sem=wsem.at[1, i], recv_sem=wsem.at[2, i],
            device_id=sibling, device_id_type=MESH,
        )
        for i, (src, dst) in enumerate(weights)
    ]
    from_sibling = [
        pltpu.make_async_remote_copy(
            src_ref=src, dst_ref=dst.at[1 - core], send_sem=wsem.at[1, i],
            recv_sem=wsem.at[2, i], device_id=sibling, device_id_type=MESH,
        )
        for i, (src, dst) in enumerate(weights)
    ]

    def dispatch(s, k):
        p = lax.rem(me + k, chips)
        return pltpu.make_async_remote_copy(
            src_ref=xs_hbm.at[s, blk(p)], dst_ref=recv.at[s, blk(me)],
            send_sem=dsend.at[s, k], recv_sem=drecv.at[s, me],
            device_id=dev(p), device_id_type=MESH,
        )

    def dispatch_in(s, k):
        q = lax.rem(me + chips - k, chips)
        return pltpu.make_async_remote_copy(
            src_ref=xs_hbm.at[s, blk(q)], dst_ref=recv.at[s, blk(q)],
            send_sem=dsend.at[s, k], recv_sem=drecv.at[s, q],
            device_id=dev(q), device_id_type=MESH,
        )

    def back(s, k):
        p = lax.rem(me + k, chips)
        return pltpu.make_async_remote_copy(
            src_ref=res.at[s, blk(p)], dst_ref=ys.at[s, blk(me)],
            send_sem=rsend.at[s, k], recv_sem=rrecv.at[s, me],
            device_id=dev(p), device_id_type=MESH,
        )

    def back_in(s, k):
        q = lax.rem(me + chips - k, chips)
        return pltpu.make_async_remote_copy(
            src_ref=res.at[s, blk(q)], dst_ref=ys.at[s, blk(q)],
            send_sem=rsend.at[s, k], recv_sem=rrecv.at[s, q],
            device_id=dev(q), device_id_type=MESH,
        )

    local_in = [
        pltpu.make_async_copy(xs_hbm.at[s, blk(me)], recv.at[s, blk(me)], lsem.at[0, s])
        for s in range(streams)
    ]
    local_out = [
        pltpu.make_async_copy(res.at[s, blk(me)], ys.at[s, blk(me)], lsem.at[1, s])
        for s in range(streams)
    ]
    for s in range(streams):
        local_in[s].start()
        for k in range(1, chips):
            dispatch(s, k).start()
    for c in to_sibling:
        c.start()
    for c in own_copies:
        c.wait()
    for c in from_sibling:
        c.wait_recv()
    for c in to_sibling:
        c.wait_send()

    tile = 128
    for s in range(streams):
        local_in[s].wait()
        for k in range(1, chips):
            dispatch_in(s, k).wait_recv()
        for b in range(rows // tile):
            x = recv[s, pl.ds(b * tile, tile), :]
            total = None
            for j in range(2):
                gate_val = jnp.dot(x, wg[j], preferred_element_type=jnp.float32)
                up_val = jnp.dot(x, wu[j], preferred_element_type=jnp.float32)
                hidden = (jax.nn.silu(gate_val) * up_val).astype(jnp.bfloat16)
                part = jnp.dot(hidden, wd[j], preferred_element_type=jnp.float32)
                part = part.astype(jnp.bfloat16).astype(jnp.float32)
                total = part if total is None else total + part
            res[s, pl.ds(b * tile, tile), :] = total.astype(jnp.bfloat16)
        local_out[s].start()
        for k in range(1, chips):
            back(s, k).start()

    for s in range(streams):
        for k in range(1, chips):
            dispatch(s, k).wait_send()
    relay = []
    for s in range(streams):
        local_out[s].wait()
        for k in range(1, chips):
            back_in(s, k).wait_recv()
        rows_back = ys[s]
        total = state_ref[s].astype(jnp.float32)
        total = total + jnp.dot(hi_ref[s], rows_back, preferred_element_type=jnp.float32)
        total = total + jnp.dot(lo_ref[s], rows_back, preferred_element_type=jnp.float32)
        mixed[s] = total.astype(jnp.bfloat16)
        send = pltpu.make_async_remote_copy(
            src_ref=mixed.at[s], dst_ref=next_hbm.at[s], send_sem=psem.at[0, s],
            recv_sem=psem.at[1, s], device_id=(section[s], me, core), device_id_type=MESH,
        )
        send.start()
        relay.append(send)
    for s in range(streams):
        for k in range(1, chips):
            back(s, k).wait_send()
    for send in relay:
        send.wait()


def expert_pass(outgoing, gate_half, up_half, down_half, state, comb_hi, comb_lo):
    streams, rows, width = outgoing.shape
    chips = lax.axis_size("ez")
    hbm = pl.BlockSpec(memory_space=pl.ANY)
    vmem = pl.BlockSpec(memory_space=pltpu.VMEM)
    return pl.pallas_call(
        functools.partial(moe_kernel, chips),
        out_shape=jax.ShapeDtypeStruct(state.shape, jnp.bfloat16),
        in_specs=[hbm] * 4 + [vmem] * 3,
        out_specs=hbm,
        scratch_shapes=[
            pltpu.VMEM(outgoing.shape, jnp.bfloat16),
            pltpu.VMEM(outgoing.shape, jnp.bfloat16),
            pltpu.VMEM(outgoing.shape, jnp.bfloat16),
            pltpu.VMEM(state.shape, jnp.bfloat16),
            pltpu.VMEM((2,) + gate_half.shape, jnp.bfloat16),
            pltpu.VMEM((2,) + up_half.shape, jnp.bfloat16),
            pltpu.VMEM((2,) + down_half.shape, jnp.bfloat16),
            pltpu.SemaphoreType.DMA((streams, chips)),
            pltpu.SemaphoreType.DMA((streams, chips)),
            pltpu.SemaphoreType.DMA((streams, chips)),
            pltpu.SemaphoreType.DMA((streams, chips)),
            pltpu.SemaphoreType.DMA((2, streams)),
            pltpu.SemaphoreType.DMA((3, 3)),
            pltpu.SemaphoreType.DMA((2, streams)),
        ],
        compiler_params=pltpu.CompilerParams(
            collective_id=0, has_side_effects=True, vmem_limit_bytes=62 * 1024 * 1024
        ),
    )(outgoing, gate_half, up_half, down_half, state, comb_hi, comb_lo)


def body(streams, norm_gain, w_gate, w_up, w_down, routes, gate_weights):
    experts = lax.axis_size("ez")
    gain_row = norm_gain[0]
    tok_rows = streams.shape[2]
    width = streams.shape[3]
    top_count = routes.shape[3]
    capacity = 2 * tok_rows * top_count // experts
    lane_count = experts * capacity
    lane_index = jnp.arange(lane_count, dtype=jnp.int32)
    expert_index = jnp.arange(experts, dtype=jnp.int32)
    outgoings, combines = [], []
    for stream in range(2):
        state = streams[0, stream].astype(jnp.float32)
        normed = (
            state * lax.rsqrt(jnp.mean(state * state, axis=-1, keepdims=True) + 1e-06) * gain_row
        ).astype(jnp.bfloat16)
        chosen = routes[0, stream].reshape(-1)
        onehot = (chosen[:, None] == expert_index[None, :]).astype(jnp.int32)
        slot_rank = jnp.sum((jnp.cumsum(onehot, axis=0) - onehot) * onehot, axis=1)
        lane_of = chosen * capacity + slot_rank
        matches = lane_index[:, None] == lane_of[None, :]
        send_matrix = jnp.sum(
            matches.reshape(lane_count, tok_rows, top_count).astype(jnp.float32), axis=-1
        ).astype(jnp.bfloat16)
        outgoing = jnp.dot(send_matrix, normed, preferred_element_type=jnp.float32).astype(
            jnp.bfloat16
        )
        weights = gate_weights[0, stream].reshape(-1)
        combine = jnp.sum(
            (matches.astype(jnp.float32) * weights[None, :]).reshape(
                lane_count, tok_rows, top_count
            ),
            axis=-1,
        ).T
        outgoings.append(outgoing)
        combines.append(combine)
    combine = jnp.stack(combines)
    comb_hi = combine.astype(jnp.bfloat16)
    comb_lo = (combine - comb_hi.astype(jnp.float32)).astype(jnp.bfloat16)
    relayed = expert_pass(
        jnp.stack(outgoings), w_gate[0, 0], w_up[0, 0], w_down[0, 0],
        streams[0], comb_hi, comb_lo,
    )
    return relayed[None]


def solution(mesh):
    pipe_size, expert_size = mesh.devices.shape
    split = Mesh(
        np.asarray(mesh.devices).reshape(pipe_size, expert_size // 2, 2), ("pipe", "ez", "ec")
    )
    tok = ("ez", "ec")
    return jax.shard_map(
        body,
        mesh=split,
        in_specs=(
            P("pipe", None, tok, None),
            P("pipe", None),
            P("pipe", tok, None, None),
            P("pipe", tok, None, None),
            P("pipe", tok, None, None),
            P("pipe", None, tok, None),
            P("pipe", None, tok, None),
        ),
        out_specs=P("pipe", None, tok, None),
        check_vma=False,
    )
```

```python
import functools

import jax
import jax.numpy as jnp
import numpy as np
from jax import lax
from jax.experimental import pallas as pl
from jax.experimental.pallas import tpu as pltpu
from jax.sharding import Mesh
from jax.sharding import PartitionSpec as P


def from_behind(value, axis, steps):
    count = lax.axis_size(axis)
    pairs = [(source, (source + steps) % count) for source in range(count)]
    return lax.ppermute(value, axis, pairs)


MESH = pl.DeviceIdType.MESH


def moe_kernel(
    chips, xs_hbm, wg_hbm, wu_hbm, wd_hbm, state_ref, hi_ref, lo_ref, next_hbm,
    recv, res, ys, mixed, wg, wu, wd, dsend, drecv, rsend, rrecv, lsem, wsem, psem,
):
    streams, rows, width = recv.shape
    cap = rows // chips
    pipe = lax.axis_index("pipe")
    pipes = lax.axis_size("pipe")
    me = lax.axis_index("ez")
    core = lax.axis_index("ec")

    def dev(p):
        return (pipe, p, core)

    def blk(p):
        return pl.ds(pl.multiple_of(p * cap, cap), cap)

    sibling = (pipe, me, 1 - core)
    weights = ((wg_hbm, wg), (wu_hbm, wu), (wd_hbm, wd))
    own_copies = [
        pltpu.make_async_copy(src, dst.at[core], wsem.at[0, i])
        for i, (src, dst) in enumerate(weights)
    ]
    for c in own_copies:
        c.start()

    barrier = pltpu.get_barrier_semaphore()
    for k in range(1, chips):
        pl.semaphore_signal(
            barrier, inc=1, device_id=dev(lax.rem(me + k, chips)), device_id_type=MESH
        )
    pl.semaphore_signal(barrier, inc=1, device_id=sibling, device_id_type=MESH)
    section = (lax.rem(pipe + 1, pipes), lax.rem(pipe + pipes - 1, pipes))
    for p in section:
        pl.semaphore_signal(barrier, inc=1, device_id=(p, me, core), device_id_type=MESH)
    pl.semaphore_wait(barrier, chips + 2)

    to_sibling = [
        pltpu.make_async_remote_copy(
            src_ref=src, dst_ref=dst.at[core], send_sem=wsem.at[1, i], recv_sem=wsem.at[2, i],
            device_id=sibling, device_id_type=MESH,
        )
        for i, (src, dst) in enumerate(weights)
    ]
    from_sibling = [
        pltpu.make_async_remote_copy(
            src_ref=src, dst_ref=dst.at[1 - core], send_sem=wsem.at[1, i],
            recv_sem=wsem.at[2, i], device_id=sibling, device_id_type=MESH,
        )
        for i, (src, dst) in enumerate(weights)
    ]

    def dispatch(s, k):
        p = lax.rem(me + k, chips)
        return pltpu.make_async_remote_copy(
            src_ref=xs_hbm.at[s, blk(p)], dst_ref=recv.at[s, blk(me)],
            send_sem=dsend.at[s, k], recv_sem=drecv.at[s, me],
            device_id=dev(p), device_id_type=MESH,
        )

    def dispatch_in(s, k):
        q = lax.rem(me + chips - k, chips)
        return pltpu.make_async_remote_copy(
            src_ref=xs_hbm.at[s, blk(q)], dst_ref=recv.at[s, blk(q)],
            send_sem=dsend.at[s, k], recv_sem=drecv.at[s, q],
            device_id=dev(q), device_id_type=MESH,
        )

    def back(s, k):
        p = lax.rem(me + k, chips)
        return pltpu.make_async_remote_copy(
            src_ref=res.at[s, blk(p)], dst_ref=ys.at[s, blk(me)],
            send_sem=rsend.at[s, k], recv_sem=rrecv.at[s, me],
            device_id=dev(p), device_id_type=MESH,
        )

    def back_in(s, k):
        q = lax.rem(me + chips - k, chips)
        return pltpu.make_async_remote_copy(
            src_ref=res.at[s, blk(q)], dst_ref=ys.at[s, blk(q)],
            send_sem=rsend.at[s, k], recv_sem=rrecv.at[s, q],
            device_id=dev(q), device_id_type=MESH,
        )

    local_in = [
        pltpu.make_async_copy(xs_hbm.at[s, blk(me)], recv.at[s, blk(me)], lsem.at[0, s])
        for s in range(streams)
    ]
    local_out = [
        pltpu.make_async_copy(res.at[s, blk(me)], ys.at[s, blk(me)], lsem.at[1, s])
        for s in range(streams)
    ]
    def send_rows(s):
        local_in[s].start()
        for k in range(1, chips):
            dispatch(s, k).start()

    def rows_arrived(s):
        local_in[s].wait()
        for k in range(1, chips):
            dispatch_in(s, k).wait_recv()

    send_rows(0)
    for c in to_sibling:
        c.start()
    for c in own_copies:
        c.wait()
    for c in from_sibling:
        c.wait_recv()
    for c in to_sibling:
        c.wait_send()

    tile = 128
    rows_arrived(0)
    for s in range(streams):
        if s + 1 < streams:
            send_rows(s + 1)
        if s > 0:
            rows_arrived(s)
        for b in range(rows // tile):
            x = recv[s, pl.ds(b * tile, tile), :]
            total = None
            for j in range(2):
                gate_val = jnp.dot(x, wg[j], preferred_element_type=jnp.float32)
                up_val = jnp.dot(x, wu[j], preferred_element_type=jnp.float32)
                hidden = (jax.nn.silu(gate_val) * up_val).astype(jnp.bfloat16)
                part = jnp.dot(hidden, wd[j], preferred_element_type=jnp.float32)
                part = part.astype(jnp.bfloat16).astype(jnp.float32)
                total = part if total is None else total + part
            res[s, pl.ds(b * tile, tile), :] = total.astype(jnp.bfloat16)
        local_out[s].start()
        for k in range(1, chips):
            back(s, k).start()

    for s in range(streams):
        for k in range(1, chips):
            dispatch(s, k).wait_send()
    relay = []
    for s in range(streams):
        local_out[s].wait()
        for k in range(1, chips):
            back_in(s, k).wait_recv()
        rows_back = ys[s]
        total = state_ref[s].astype(jnp.float32)
        total = total + jnp.dot(hi_ref[s], rows_back, preferred_element_type=jnp.float32)
        total = total + jnp.dot(lo_ref[s], rows_back, preferred_element_type=jnp.float32)
        mixed[s] = total.astype(jnp.bfloat16)
        send = pltpu.make_async_remote_copy(
            src_ref=mixed.at[s], dst_ref=next_hbm.at[s], send_sem=psem.at[0, s],
            recv_sem=psem.at[1, s], device_id=(section[s], me, core), device_id_type=MESH,
        )
        send.start()
        relay.append(send)
    for s in range(streams):
        for k in range(1, chips):
            back(s, k).wait_send()
    for send in relay:
        send.wait()


def expert_pass(outgoing, gate_half, up_half, down_half, state, comb_hi, comb_lo):
    streams, rows, width = outgoing.shape
    chips = lax.axis_size("ez")
    hbm = pl.BlockSpec(memory_space=pl.ANY)
    vmem = pl.BlockSpec(memory_space=pltpu.VMEM)
    return pl.pallas_call(
        functools.partial(moe_kernel, chips),
        out_shape=jax.ShapeDtypeStruct(state.shape, jnp.bfloat16),
        in_specs=[hbm] * 4 + [vmem] * 3,
        out_specs=hbm,
        scratch_shapes=[
            pltpu.VMEM(outgoing.shape, jnp.bfloat16),
            pltpu.VMEM(outgoing.shape, jnp.bfloat16),
            pltpu.VMEM(outgoing.shape, jnp.bfloat16),
            pltpu.VMEM(state.shape, jnp.bfloat16),
            pltpu.VMEM((2,) + gate_half.shape, jnp.bfloat16),
            pltpu.VMEM((2,) + up_half.shape, jnp.bfloat16),
            pltpu.VMEM((2,) + down_half.shape, jnp.bfloat16),
            pltpu.SemaphoreType.DMA((streams, chips)),
            pltpu.SemaphoreType.DMA((streams, chips)),
            pltpu.SemaphoreType.DMA((streams, chips)),
            pltpu.SemaphoreType.DMA((streams, chips)),
            pltpu.SemaphoreType.DMA((2, streams)),
            pltpu.SemaphoreType.DMA((3, 3)),
            pltpu.SemaphoreType.DMA((2, streams)),
        ],
        compiler_params=pltpu.CompilerParams(
            collective_id=0, has_side_effects=True, vmem_limit_bytes=62 * 1024 * 1024
        ),
    )(outgoing, gate_half, up_half, down_half, state, comb_hi, comb_lo)


def body(streams, norm_gain, w_gate, w_up, w_down, routes, gate_weights):
    experts = lax.axis_size("ez")
    gain_row = norm_gain[0]
    tok_rows = streams.shape[2]
    width = streams.shape[3]
    top_count = routes.shape[3]
    capacity = 2 * tok_rows * top_count // experts
    lane_count = experts * capacity
    lane_index = jnp.arange(lane_count, dtype=jnp.int32)
    expert_index = jnp.arange(experts, dtype=jnp.int32)
    outgoings, combines = [], []
    for stream in range(2):
        state = streams[0, stream].astype(jnp.float32)
        normed = (
            state * lax.rsqrt(jnp.mean(state * state, axis=-1, keepdims=True) + 1e-06) * gain_row
        ).astype(jnp.bfloat16)
        chosen = routes[0, stream].reshape(-1)
        onehot = (chosen[:, None] == expert_index[None, :]).astype(jnp.int32)
        slot_rank = jnp.sum((jnp.cumsum(onehot, axis=0) - onehot) * onehot, axis=1)
        lane_of = chosen * capacity + slot_rank
        matches = lane_index[:, None] == lane_of[None, :]
        send_matrix = jnp.sum(
            matches.reshape(lane_count, tok_rows, top_count).astype(jnp.float32), axis=-1
        ).astype(jnp.bfloat16)
        outgoing = jnp.dot(send_matrix, normed, preferred_element_type=jnp.float32).astype(
            jnp.bfloat16
        )
        weights = gate_weights[0, stream].reshape(-1)
        combine = jnp.sum(
            (matches.astype(jnp.float32) * weights[None, :]).reshape(
                lane_count, tok_rows, top_count
            ),
            axis=-1,
        ).T
        outgoings.append(outgoing)
        combines.append(combine)
    combine = jnp.stack(combines)
    comb_hi = combine.astype(jnp.bfloat16)
    comb_lo = (combine - comb_hi.astype(jnp.float32)).astype(jnp.bfloat16)
    relayed = expert_pass(
        jnp.stack(outgoings), w_gate[0, 0], w_up[0, 0], w_down[0, 0],
        streams[0], comb_hi, comb_lo,
    )
    return relayed[None]


def solution(mesh):
    pipe_size, expert_size = mesh.devices.shape
    split = Mesh(
        np.asarray(mesh.devices).reshape(pipe_size, expert_size // 2, 2), ("pipe", "ez", "ec")
    )
    tok = ("ez", "ec")
    return jax.shard_map(
        body,
        mesh=split,
        in_specs=(
            P("pipe", None, tok, None),
            P("pipe", None),
            P("pipe", tok, None, None),
            P("pipe", tok, None, None),
            P("pipe", tok, None, None),
            P("pipe", None, tok, None),
            P("pipe", None, tok, None),
        ),
        out_specs=P("pipe", None, tok, None),
        check_vma=False,
    )
```

```python
import functools

import jax
import jax.numpy as jnp
import numpy as np
from jax import lax
from jax.experimental import pallas as pl
from jax.experimental.pallas import tpu as pltpu
from jax.sharding import Mesh
from jax.sharding import PartitionSpec as P


def from_behind(value, axis, steps):
    count = lax.axis_size(axis)
    pairs = [(source, (source + steps) % count) for source in range(count)]
    return lax.ppermute(value, axis, pairs)


MESH = pl.DeviceIdType.MESH


def moe_kernel(
    chips, xs_hbm, wg_hbm, wu_hbm, wd_hbm, state_ref, hi_ref, lo_ref, next_hbm,
    recv, res, ys, mixed, rbuf, wg, wu, wd, dsend, drecv, rsend, rrecv, lsem, wsem, psem, rsem,
):
    streams, rows, width = recv.shape
    cap = rows // chips
    pipe = lax.axis_index("pipe")
    pipes = lax.axis_size("pipe")
    me = lax.axis_index("ez")
    core = lax.axis_index("ec")

    def dev(p):
        return (pipe, p, core)

    def blk(p):
        return pl.ds(pl.multiple_of(p * cap, cap), cap)

    sibling = (pipe, me, 1 - core)
    weights = ((wg_hbm, wg), (wu_hbm, wu), (wd_hbm, wd))
    own_copies = [
        pltpu.make_async_copy(src, dst.at[core], wsem.at[0, i])
        for i, (src, dst) in enumerate(weights)
    ]
    for c in own_copies:
        c.start()

    barrier = pltpu.get_barrier_semaphore()
    for k in range(1, chips):
        pl.semaphore_signal(
            barrier, inc=1, device_id=dev(lax.rem(me + k, chips)), device_id_type=MESH
        )
    pl.semaphore_signal(barrier, inc=1, device_id=sibling, device_id_type=MESH)
    section = (lax.rem(pipe + 1, pipes), lax.rem(pipe + pipes - 1, pipes))
    for p in section:
        pl.semaphore_signal(barrier, inc=1, device_id=(p, me, core), device_id_type=MESH)
    pl.semaphore_wait(barrier, chips + 2)

    to_sibling = [
        pltpu.make_async_remote_copy(
            src_ref=src, dst_ref=dst.at[core], send_sem=wsem.at[1, i], recv_sem=wsem.at[2, i],
            device_id=sibling, device_id_type=MESH,
        )
        for i, (src, dst) in enumerate(weights)
    ]
    from_sibling = [
        pltpu.make_async_remote_copy(
            src_ref=src, dst_ref=dst.at[1 - core], send_sem=wsem.at[1, i],
            recv_sem=wsem.at[2, i], device_id=sibling, device_id_type=MESH,
        )
        for i, (src, dst) in enumerate(weights)
    ]

    def dispatch(s, k):
        p = lax.rem(me + k, chips)
        return pltpu.make_async_remote_copy(
            src_ref=xs_hbm.at[s, blk(p)], dst_ref=recv.at[s, blk(me)],
            send_sem=dsend.at[s, k], recv_sem=drecv.at[s, me],
            device_id=dev(p), device_id_type=MESH,
        )

    def dispatch_in(s, k):
        q = lax.rem(me + chips - k, chips)
        return pltpu.make_async_remote_copy(
            src_ref=xs_hbm.at[s, blk(q)], dst_ref=recv.at[s, blk(q)],
            send_sem=dsend.at[s, k], recv_sem=drecv.at[s, q],
            device_id=dev(q), device_id_type=MESH,
        )

    def back(s, k):
        p = lax.rem(me + k, chips)
        return pltpu.make_async_remote_copy(
            src_ref=res.at[s, blk(p)], dst_ref=ys.at[s, blk(me)],
            send_sem=rsend.at[s, k], recv_sem=rrecv.at[s, me],
            device_id=dev(p), device_id_type=MESH,
        )

    def back_in(s, k):
        q = lax.rem(me + chips - k, chips)
        return pltpu.make_async_remote_copy(
            src_ref=res.at[s, blk(q)], dst_ref=ys.at[s, blk(q)],
            send_sem=rsend.at[s, k], recv_sem=rrecv.at[s, q],
            device_id=dev(q), device_id_type=MESH,
        )

    anti = chips // 2
    half = cap // 2
    send_from = (xs_hbm, res)
    land_in = (recv, ys)

    def half_rows(q, h):
        return pl.ds(pl.multiple_of(q * cap + h * half, half), half)

    def via(h):
        return lax.rem(me + (anti - 1 if h == 0 else chips - anti + 1), chips)

    def relay_out(ph, s, h):
        return pltpu.make_async_remote_copy(
            src_ref=send_from[ph].at[s, half_rows(lax.rem(me + anti, chips), h)],
            dst_ref=rbuf.at[ph, s, h], send_sem=rsem.at[0, ph, s, h],
            recv_sem=rsem.at[1, ph, s, h], device_id=dev(via(h)), device_id_type=MESH,
        )

    def forward(ph, s, h):
        step = 1 if h == 0 else chips - 1
        origin = lax.rem(me + chips - anti + 1, chips) if h == 0 else lax.rem(me + anti - 1, chips)
        return pltpu.make_async_remote_copy(
            src_ref=rbuf.at[ph, s, h], dst_ref=land_in[ph].at[s, half_rows(origin, h)],
            send_sem=rsem.at[2, ph, s, h], recv_sem=rsem.at[3, ph, s, h],
            device_id=dev(lax.rem(me + step, chips)), device_id_type=MESH,
        )

    def forward_in(ph, s, h):
        origin = lax.rem(me + anti, chips)
        return pltpu.make_async_remote_copy(
            src_ref=rbuf.at[ph, s, h], dst_ref=land_in[ph].at[s, half_rows(origin, h)],
            send_sem=rsem.at[2, ph, s, h], recv_sem=rsem.at[3, ph, s, h],
            device_id=dev(origin), device_id_type=MESH,
        )

    def relay_start(ph, s):
        for h in range(2):
            relay_out(ph, s, h).start()

    def relay_pass_on(ph, s):
        for h in range(2):
            relay_out(ph, s, h).wait_recv()
            forward(ph, s, h).start()

    def relay_landed(ph, s):
        for h in range(2):
            forward_in(ph, s, h).wait_recv()

    def relay_done(ph, s):
        for h in range(2):
            relay_out(ph, s, h).wait_send()
            forward(ph, s, h).wait_send()

    direct = [k for k in range(1, chips) if k != anti]

    local_in = [
        pltpu.make_async_copy(xs_hbm.at[s, blk(me)], recv.at[s, blk(me)], lsem.at[0, s])
        for s in range(streams)
    ]
    local_out = [
        pltpu.make_async_copy(res.at[s, blk(me)], ys.at[s, blk(me)], lsem.at[1, s])
        for s in range(streams)
    ]
    def send_rows(s):
        local_in[s].start()
        relay_start(0, s)
        for k in direct:
            dispatch(s, k).start()

    def rows_arrived(s):
        relay_pass_on(0, s)
        local_in[s].wait()
        for k in direct:
            dispatch_in(s, k).wait_recv()
        relay_landed(0, s)

    for s in range(streams):
        send_rows(s)
    for c in to_sibling:
        c.start()
    for c in own_copies:
        c.wait()
    for c in from_sibling:
        c.wait_recv()
    for c in to_sibling:
        c.wait_send()

    tile = 128
    for s in range(streams):
        rows_arrived(s)
        for b in range(rows // tile):
            x = recv[s, pl.ds(b * tile, tile), :]
            total = None
            for j in range(2):
                gate_val = jnp.dot(x, wg[j], preferred_element_type=jnp.float32)
                up_val = jnp.dot(x, wu[j], preferred_element_type=jnp.float32)
                hidden = (jax.nn.silu(gate_val) * up_val).astype(jnp.bfloat16)
                part = jnp.dot(hidden, wd[j], preferred_element_type=jnp.float32)
                part = part.astype(jnp.bfloat16).astype(jnp.float32)
                total = part if total is None else total + part
            res[s, pl.ds(b * tile, tile), :] = total.astype(jnp.bfloat16)
        local_out[s].start()
        relay_start(1, s)
        for k in direct:
            back(s, k).start()

    for s in range(streams):
        for k in direct:
            dispatch(s, k).wait_send()
    relay = []
    for s in range(streams):
        relay_pass_on(1, s)
        local_out[s].wait()
        for k in direct:
            back_in(s, k).wait_recv()
        relay_landed(1, s)
        rows_back = ys[s]
        total = state_ref[s].astype(jnp.float32)
        total = total + jnp.dot(hi_ref[s], rows_back, preferred_element_type=jnp.float32)
        total = total + jnp.dot(lo_ref[s], rows_back, preferred_element_type=jnp.float32)
        mixed[s] = total.astype(jnp.bfloat16)
        send = pltpu.make_async_remote_copy(
            src_ref=mixed.at[s], dst_ref=next_hbm.at[s], send_sem=psem.at[0, s],
            recv_sem=psem.at[1, s], device_id=(section[s], me, core), device_id_type=MESH,
        )
        send.start()
        relay.append(send)
    for s in range(streams):
        for k in direct:
            back(s, k).wait_send()
        for ph in range(2):
            relay_done(ph, s)
    for send in relay:
        send.wait()


def expert_pass(outgoing, gate_half, up_half, down_half, state, comb_hi, comb_lo):
    streams, rows, width = outgoing.shape
    chips = lax.axis_size("ez")
    hbm = pl.BlockSpec(memory_space=pl.ANY)
    vmem = pl.BlockSpec(memory_space=pltpu.VMEM)
    return pl.pallas_call(
        functools.partial(moe_kernel, chips),
        out_shape=jax.ShapeDtypeStruct(state.shape, jnp.bfloat16),
        in_specs=[hbm] * 4 + [vmem] * 3,
        out_specs=hbm,
        scratch_shapes=[
            pltpu.VMEM(outgoing.shape, jnp.bfloat16),
            pltpu.VMEM(outgoing.shape, jnp.bfloat16),
            pltpu.VMEM(outgoing.shape, jnp.bfloat16),
            pltpu.VMEM(state.shape, jnp.bfloat16),
            pltpu.VMEM((2, streams, 2, rows // chips // 2, width), jnp.bfloat16),
            pltpu.VMEM((2,) + gate_half.shape, jnp.bfloat16),
            pltpu.VMEM((2,) + up_half.shape, jnp.bfloat16),
            pltpu.VMEM((2,) + down_half.shape, jnp.bfloat16),
            pltpu.SemaphoreType.DMA((streams, chips)),
            pltpu.SemaphoreType.DMA((streams, chips)),
            pltpu.SemaphoreType.DMA((streams, chips)),
            pltpu.SemaphoreType.DMA((streams, chips)),
            pltpu.SemaphoreType.DMA((2, streams)),
            pltpu.SemaphoreType.DMA((3, 3)),
            pltpu.SemaphoreType.DMA((2, streams)),
            pltpu.SemaphoreType.DMA((4, 2, streams, 2)),
        ],
        compiler_params=pltpu.CompilerParams(
            collective_id=0, has_side_effects=True, vmem_limit_bytes=62 * 1024 * 1024
        ),
    )(outgoing, gate_half, up_half, down_half, state, comb_hi, comb_lo)


def body(streams, norm_gain, w_gate, w_up, w_down, routes, gate_weights):
    experts = lax.axis_size("ez")
    gain_row = norm_gain[0]
    tok_rows = streams.shape[2]
    width = streams.shape[3]
    top_count = routes.shape[3]
    capacity = 2 * tok_rows * top_count // experts
    lane_count = experts * capacity
    lane_index = jnp.arange(lane_count, dtype=jnp.int32)
    expert_index = jnp.arange(experts, dtype=jnp.int32)
    outgoings, combines = [], []
    for stream in range(2):
        state = streams[0, stream].astype(jnp.float32)
        normed = (
            state * lax.rsqrt(jnp.mean(state * state, axis=-1, keepdims=True) + 1e-06) * gain_row
        ).astype(jnp.bfloat16)
        chosen = routes[0, stream].reshape(-1)
        onehot = (chosen[:, None] == expert_index[None, :]).astype(jnp.int32)
        slot_rank = jnp.sum((jnp.cumsum(onehot, axis=0) - onehot) * onehot, axis=1)
        lane_of = chosen * capacity + slot_rank
        matches = lane_index[:, None] == lane_of[None, :]
        send_matrix = jnp.sum(
            matches.reshape(lane_count, tok_rows, top_count).astype(jnp.float32), axis=-1
        ).astype(jnp.bfloat16)
        outgoing = jnp.dot(send_matrix, normed, preferred_element_type=jnp.float32).astype(
            jnp.bfloat16
        )
        weights = gate_weights[0, stream].reshape(-1)
        combine = jnp.sum(
            (matches.astype(jnp.float32) * weights[None, :]).reshape(
                lane_count, tok_rows, top_count
            ),
            axis=-1,
        ).T
        outgoings.append(outgoing)
        combines.append(combine)
    combine = jnp.stack(combines)
    comb_hi = combine.astype(jnp.bfloat16)
    comb_lo = (combine - comb_hi.astype(jnp.float32)).astype(jnp.bfloat16)
    relayed = expert_pass(
        jnp.stack(outgoings), w_gate[0, 0], w_up[0, 0], w_down[0, 0],
        streams[0], comb_hi, comb_lo,
    )
    return relayed[None]


def solution(mesh):
    pipe_size, expert_size = mesh.devices.shape
    split = Mesh(
        np.asarray(mesh.devices).reshape(pipe_size, expert_size // 2, 2), ("pipe", "ez", "ec")
    )
    tok = ("ez", "ec")
    return jax.shard_map(
        body,
        mesh=split,
        in_specs=(
            P("pipe", None, tok, None),
            P("pipe", None),
            P("pipe", tok, None, None),
            P("pipe", tok, None, None),
            P("pipe", tok, None, None),
            P("pipe", None, tok, None),
            P("pipe", None, tok, None),
        ),
        out_specs=P("pipe", None, tok, None),
        check_vma=False,
    )
```

```python
import functools

import jax
import jax.numpy as jnp
import numpy as np
from jax import lax
from jax.experimental import pallas as pl
from jax.experimental.pallas import tpu as pltpu
from jax.sharding import Mesh
from jax.sharding import PartitionSpec as P


def from_behind(value, axis, steps):
    count = lax.axis_size(axis)
    pairs = [(source, (source + steps) % count) for source in range(count)]
    return lax.ppermute(value, axis, pairs)


MESH = pl.DeviceIdType.MESH


def moe_kernel(
    chips, wg_hbm, wu_hbm, wd_hbm, state_ref, gain_ref, pick_ref, hi_ref, lo_ref, next_hbm,
    xs, recv, res, ys, mixed, wg, wu, wd, dsend, drecv, rsend, rrecv, lsem, wsem, psem,
):
    streams, rows, width = recv.shape
    cap = rows // chips
    pipe = lax.axis_index("pipe")
    pipes = lax.axis_size("pipe")
    me = lax.axis_index("ez")
    core = lax.axis_index("ec")

    def dev(p):
        return (pipe, p, core)

    def blk(p):
        return pl.ds(pl.multiple_of(p * cap, cap), cap)

    sibling = (pipe, me, 1 - core)
    weights = ((wg_hbm, wg), (wu_hbm, wu), (wd_hbm, wd))
    own_copies = [
        pltpu.make_async_copy(src, dst.at[core], wsem.at[0, i])
        for i, (src, dst) in enumerate(weights)
    ]
    for c in own_copies:
        c.start()

    barrier = pltpu.get_barrier_semaphore()
    for k in range(1, chips):
        pl.semaphore_signal(
            barrier, inc=1, device_id=dev(lax.rem(me + k, chips)), device_id_type=MESH
        )
    pl.semaphore_signal(barrier, inc=1, device_id=sibling, device_id_type=MESH)
    section = (lax.rem(pipe + 1, pipes), lax.rem(pipe + pipes - 1, pipes))
    for p in section:
        pl.semaphore_signal(barrier, inc=1, device_id=(p, me, core), device_id_type=MESH)
    pl.semaphore_wait(barrier, chips + 2)

    to_sibling = [
        pltpu.make_async_remote_copy(
            src_ref=src, dst_ref=dst.at[core], send_sem=wsem.at[1, i], recv_sem=wsem.at[2, i],
            device_id=sibling, device_id_type=MESH,
        )
        for i, (src, dst) in enumerate(weights)
    ]
    from_sibling = [
        pltpu.make_async_remote_copy(
            src_ref=src, dst_ref=dst.at[1 - core], send_sem=wsem.at[1, i],
            recv_sem=wsem.at[2, i], device_id=sibling, device_id_type=MESH,
        )
        for i, (src, dst) in enumerate(weights)
    ]

    def dispatch(s, k):
        p = lax.rem(me + k, chips)
        return pltpu.make_async_remote_copy(
            src_ref=xs.at[s, blk(p)], dst_ref=recv.at[s, blk(me)],
            send_sem=dsend.at[s, k], recv_sem=drecv.at[s, me],
            device_id=dev(p), device_id_type=MESH,
        )

    def dispatch_in(s, k):
        q = lax.rem(me + chips - k, chips)
        return pltpu.make_async_remote_copy(
            src_ref=xs.at[s, blk(q)], dst_ref=recv.at[s, blk(q)],
            send_sem=dsend.at[s, k], recv_sem=drecv.at[s, q],
            device_id=dev(q), device_id_type=MESH,
        )

    def back(s, k):
        p = lax.rem(me + k, chips)
        return pltpu.make_async_remote_copy(
            src_ref=res.at[s, blk(p)], dst_ref=ys.at[s, blk(me)],
            send_sem=rsend.at[s, k], recv_sem=rrecv.at[s, me],
            device_id=dev(p), device_id_type=MESH,
        )

    def back_in(s, k):
        q = lax.rem(me + chips - k, chips)
        return pltpu.make_async_remote_copy(
            src_ref=res.at[s, blk(q)], dst_ref=ys.at[s, blk(q)],
            send_sem=rsend.at[s, k], recv_sem=rrecv.at[s, q],
            device_id=dev(q), device_id_type=MESH,
        )

    local_in = [
        pltpu.make_async_copy(xs.at[s, blk(me)], recv.at[s, blk(me)], lsem.at[0, s])
        for s in range(streams)
    ]
    local_out = [
        pltpu.make_async_copy(res.at[s, blk(me)], ys.at[s, blk(me)], lsem.at[1, s])
        for s in range(streams)
    ]
    for s in range(streams):
        state = state_ref[s].astype(jnp.float32)
        scale = lax.rsqrt(jnp.mean(state * state, axis=-1, keepdims=True) + 1e-06)
        normed = (state * scale * gain_ref[...]).astype(jnp.bfloat16)
        xs[s] = jnp.dot(pick_ref[s], normed, preferred_element_type=jnp.float32).astype(
            jnp.bfloat16
        )
        local_in[s].start()
        for k in range(1, chips):
            dispatch(s, k).start()
    for c in to_sibling:
        c.start()
    for c in own_copies:
        c.wait()
    for c in from_sibling:
        c.wait_recv()
    for c in to_sibling:
        c.wait_send()

    tile = 128
    for s in range(streams):
        local_in[s].wait()
        for k in range(1, chips):
            dispatch_in(s, k).wait_recv()
        for b in range(rows // tile):
            x = recv[s, pl.ds(b * tile, tile), :]
            total = None
            for j in range(2):
                gate_val = jnp.dot(x, wg[j], preferred_element_type=jnp.float32)
                up_val = jnp.dot(x, wu[j], preferred_element_type=jnp.float32)
                hidden = (jax.nn.silu(gate_val) * up_val).astype(jnp.bfloat16)
                part = jnp.dot(hidden, wd[j], preferred_element_type=jnp.float32)
                part = part.astype(jnp.bfloat16).astype(jnp.float32)
                total = part if total is None else total + part
            res[s, pl.ds(b * tile, tile), :] = total.astype(jnp.bfloat16)
        local_out[s].start()
        for k in range(1, chips):
            back(s, k).start()

    for s in range(streams):
        for k in range(1, chips):
            dispatch(s, k).wait_send()
    relay = []
    for s in range(streams):
        local_out[s].wait()
        for k in range(1, chips):
            back_in(s, k).wait_recv()
        rows_back = ys[s]
        total = state_ref[s].astype(jnp.float32)
        total = total + jnp.dot(hi_ref[s], rows_back, preferred_element_type=jnp.float32)
        total = total + jnp.dot(lo_ref[s], rows_back, preferred_element_type=jnp.float32)
        mixed[s] = total.astype(jnp.bfloat16)
        send = pltpu.make_async_remote_copy(
            src_ref=mixed.at[s], dst_ref=next_hbm.at[s], send_sem=psem.at[0, s],
            recv_sem=psem.at[1, s], device_id=(section[s], me, core), device_id_type=MESH,
        )
        send.start()
        relay.append(send)
    for s in range(streams):
        for k in range(1, chips):
            back(s, k).wait_send()
    for send in relay:
        send.wait()


def expert_pass(pick, gate_half, up_half, down_half, state, gain, comb_hi, comb_lo):
    streams, rows, _ = pick.shape
    width = state.shape[-1]
    chips = lax.axis_size("ez")
    hbm = pl.BlockSpec(memory_space=pl.ANY)
    vmem = pl.BlockSpec(memory_space=pltpu.VMEM)
    lanes = (streams, rows, width)
    return pl.pallas_call(
        functools.partial(moe_kernel, chips),
        out_shape=jax.ShapeDtypeStruct(state.shape, jnp.bfloat16),
        in_specs=[hbm] * 3 + [vmem] * 5,
        out_specs=hbm,
        scratch_shapes=[
            pltpu.VMEM(lanes, jnp.bfloat16),
            pltpu.VMEM(lanes, jnp.bfloat16),
            pltpu.VMEM(lanes, jnp.bfloat16),
            pltpu.VMEM(lanes, jnp.bfloat16),
            pltpu.VMEM(state.shape, jnp.bfloat16),
            pltpu.VMEM((2,) + gate_half.shape, jnp.bfloat16),
            pltpu.VMEM((2,) + up_half.shape, jnp.bfloat16),
            pltpu.VMEM((2,) + down_half.shape, jnp.bfloat16),
            pltpu.SemaphoreType.DMA((streams, chips)),
            pltpu.SemaphoreType.DMA((streams, chips)),
            pltpu.SemaphoreType.DMA((streams, chips)),
            pltpu.SemaphoreType.DMA((streams, chips)),
            pltpu.SemaphoreType.DMA((2, streams)),
            pltpu.SemaphoreType.DMA((3, 3)),
            pltpu.SemaphoreType.DMA((2, streams)),
        ],
        compiler_params=pltpu.CompilerParams(
            collective_id=0, has_side_effects=True, vmem_limit_bytes=62 * 1024 * 1024
        ),
    )(gate_half, up_half, down_half, state, gain, pick, comb_hi, comb_lo)


def body(streams, norm_gain, w_gate, w_up, w_down, routes, gate_weights):
    experts = lax.axis_size("ez")
    tok_rows = streams.shape[2]
    width = streams.shape[3]
    top_count = routes.shape[3]
    capacity = 2 * tok_rows * top_count // experts
    lane_count = experts * capacity
    lane_index = jnp.arange(lane_count, dtype=jnp.int32)
    expert_index = jnp.arange(experts, dtype=jnp.int32)
    outgoings, combines = [], []
    for stream in range(2):
        chosen = routes[0, stream].reshape(-1)
        onehot = (chosen[:, None] == expert_index[None, :]).astype(jnp.int32)
        slot_rank = jnp.sum((jnp.cumsum(onehot, axis=0) - onehot) * onehot, axis=1)
        lane_of = chosen * capacity + slot_rank
        matches = lane_index[:, None] == lane_of[None, :]
        send_matrix = jnp.sum(
            matches.reshape(lane_count, tok_rows, top_count).astype(jnp.float32), axis=-1
        ).astype(jnp.bfloat16)
        weights = gate_weights[0, stream].reshape(-1)
        combine = jnp.sum(
            (matches.astype(jnp.float32) * weights[None, :]).reshape(
                lane_count, tok_rows, top_count
            ),
            axis=-1,
        ).T
        outgoings.append(send_matrix)
        combines.append(combine)
    combine = jnp.stack(combines)
    comb_hi = combine.astype(jnp.bfloat16)
    comb_lo = (combine - comb_hi.astype(jnp.float32)).astype(jnp.bfloat16)
    relayed = expert_pass(
        jnp.stack(outgoings), w_gate[0, 0], w_up[0, 0], w_down[0, 0],
        streams[0], norm_gain, comb_hi, comb_lo,
    )
    return relayed[None]


def solution(mesh):
    pipe_size, expert_size = mesh.devices.shape
    split = Mesh(
        np.asarray(mesh.devices).reshape(pipe_size, expert_size // 2, 2), ("pipe", "ez", "ec")
    )
    tok = ("ez", "ec")
    return jax.shard_map(
        body,
        mesh=split,
        in_specs=(
            P("pipe", None, tok, None),
            P("pipe", None),
            P("pipe", tok, None, None),
            P("pipe", tok, None, None),
            P("pipe", tok, None, None),
            P("pipe", None, tok, None),
            P("pipe", None, tok, None),
        ),
        out_specs=P("pipe", None, tok, None),
        check_vma=False,
    )
```

```python
import functools

import jax
import jax.numpy as jnp
import numpy as np
from jax import lax
from jax.experimental import pallas as pl
from jax.experimental.pallas import tpu as pltpu
from jax.sharding import Mesh
from jax.sharding import PartitionSpec as P


def from_behind(value, axis, steps):
    count = lax.axis_size(axis)
    pairs = [(source, (source + steps) % count) for source in range(count)]
    return lax.ppermute(value, axis, pairs)


MESH = pl.DeviceIdType.MESH


def moe_kernel(
    chips, wg_hbm, wu_hbm, wd_hbm, state_ref, gain_ref, pick_ref, hi_ref, lo_ref, next_hbm,
    xs, recv, res, ys, mixed, wg, wu, wd, dsend, drecv, rsend, rrecv, lsem, wsem, psem,
):
    streams, rows, width = recv.shape
    cap = rows // chips
    pipe = lax.axis_index("pipe")
    pipes = lax.axis_size("pipe")
    me = lax.axis_index("ez")
    core = lax.axis_index("ec")

    def dev(p):
        return (pipe, p, core)

    def blk(p):
        return pl.ds(pl.multiple_of(p * cap, cap), cap)

    sibling = (pipe, me, 1 - core)
    weights = ((wg_hbm, wg), (wu_hbm, wu), (wd_hbm, wd))
    own_copies = [
        pltpu.make_async_copy(src, dst.at[core], wsem.at[0, i])
        for i, (src, dst) in enumerate(weights)
    ]
    for c in own_copies:
        c.start()

    barrier = pltpu.get_barrier_semaphore()
    for k in range(1, chips):
        pl.semaphore_signal(
            barrier, inc=1, device_id=dev(lax.rem(me + k, chips)), device_id_type=MESH
        )
    pl.semaphore_signal(barrier, inc=1, device_id=sibling, device_id_type=MESH)
    section = (lax.rem(pipe + 1, pipes), lax.rem(pipe + pipes - 1, pipes))
    for p in section:
        pl.semaphore_signal(barrier, inc=1, device_id=(p, me, core), device_id_type=MESH)
    pl.semaphore_wait(barrier, chips + 2)

    to_sibling = [
        pltpu.make_async_remote_copy(
            src_ref=src, dst_ref=dst.at[core], send_sem=wsem.at[1, i], recv_sem=wsem.at[2, i],
            device_id=sibling, device_id_type=MESH,
        )
        for i, (src, dst) in enumerate(weights)
    ]
    from_sibling = [
        pltpu.make_async_remote_copy(
            src_ref=src, dst_ref=dst.at[1 - core], send_sem=wsem.at[1, i],
            recv_sem=wsem.at[2, i], device_id=sibling, device_id_type=MESH,
        )
        for i, (src, dst) in enumerate(weights)
    ]

    def dispatch(s, k):
        p = lax.rem(me + k, chips)
        return pltpu.make_async_remote_copy(
            src_ref=xs.at[s, blk(p)], dst_ref=recv.at[s, blk(me)],
            send_sem=dsend.at[s, k], recv_sem=drecv.at[s, me],
            device_id=dev(p), device_id_type=MESH,
        )

    def dispatch_in(s, k):
        q = lax.rem(me + chips - k, chips)
        return pltpu.make_async_remote_copy(
            src_ref=xs.at[s, blk(q)], dst_ref=recv.at[s, blk(q)],
            send_sem=dsend.at[s, k], recv_sem=drecv.at[s, q],
            device_id=dev(q), device_id_type=MESH,
        )

    def back(s, k):
        p = lax.rem(me + k, chips)
        return pltpu.make_async_remote_copy(
            src_ref=res.at[s, blk(p)], dst_ref=ys.at[s, blk(me)],
            send_sem=rsend.at[s, k], recv_sem=rrecv.at[s, me],
            device_id=dev(p), device_id_type=MESH,
        )

    def back_in(s, k):
        q = lax.rem(me + chips - k, chips)
        return pltpu.make_async_remote_copy(
            src_ref=res.at[s, blk(q)], dst_ref=ys.at[s, blk(q)],
            send_sem=rsend.at[s, k], recv_sem=rrecv.at[s, q],
            device_id=dev(q), device_id_type=MESH,
        )

    local_in = [
        pltpu.make_async_copy(xs.at[s, blk(me)], recv.at[s, blk(me)], lsem.at[0, s])
        for s in range(streams)
    ]
    local_out = [
        pltpu.make_async_copy(res.at[s, blk(me)], ys.at[s, blk(me)], lsem.at[1, s])
        for s in range(streams)
    ]
    for s in range(streams):
        state = state_ref[s].astype(jnp.float32)
        scale = lax.rsqrt(jnp.mean(state * state, axis=-1, keepdims=True) + 1e-06)
        normed = (state * scale * gain_ref[...]).astype(jnp.bfloat16)
        xs[s] = jnp.dot(pick_ref[s], normed, preferred_element_type=jnp.float32).astype(
            jnp.bfloat16
        )
        local_in[s].start()
        for k in range(1, chips):
            dispatch(s, k).start()
    for c in to_sibling:
        c.start()
    for c in own_copies:
        c.wait()
    for c in from_sibling:
        c.wait_recv()
    for c in to_sibling:
        c.wait_send()

    tile = 128
    for s in range(streams):
        local_in[s].wait()
        for k in range(1, chips):
            dispatch_in(s, k).wait_recv()
        for b in range(rows // tile):
            x = recv[s, pl.ds(b * tile, tile), :]
            total = None
            for j in range(2):
                gate_val = jnp.dot(x, wg[j], preferred_element_type=jnp.float32)
                up_val = jnp.dot(x, wu[j], preferred_element_type=jnp.float32)
                hidden = (jax.nn.silu(gate_val) * up_val).astype(jnp.bfloat16)
                part = jnp.dot(hidden, wd[j], preferred_element_type=jnp.float32)
                part = part.astype(jnp.bfloat16).astype(jnp.float32)
                total = part if total is None else total + part
            res[s, pl.ds(b * tile, tile), :] = total.astype(jnp.bfloat16)
        local_out[s].start()
        for k in range(1, chips):
            back(s, k).start()

    for s in range(streams):
        for k in range(1, chips):
            dispatch(s, k).wait_send()
    relay = []
    for s in range(streams):
        local_out[s].wait()
        for k in range(1, chips):
            back_in(s, k).wait_recv()
        rows_back = ys[s]
        total = state_ref[s].astype(jnp.float32)
        total = total + jnp.dot(hi_ref[s], rows_back, preferred_element_type=jnp.float32)
        total = total + jnp.dot(lo_ref[s], rows_back, preferred_element_type=jnp.float32)
        mixed[s] = total.astype(jnp.bfloat16)
        send = pltpu.make_async_remote_copy(
            src_ref=mixed.at[s], dst_ref=next_hbm.at[s], send_sem=psem.at[0, s],
            recv_sem=psem.at[1, s], device_id=(section[s], me, core), device_id_type=MESH,
        )
        send.start()
        relay.append(send)
    for s in range(streams):
        for k in range(1, chips):
            back(s, k).wait_send()
    for send in relay:
        send.wait()


def expert_pass(pick, gate_half, up_half, down_half, state, gain, comb_hi, comb_lo):
    streams, rows, _ = pick.shape
    width = state.shape[-1]
    chips = lax.axis_size("ez")
    hbm = pl.BlockSpec(memory_space=pl.ANY)
    vmem = pl.BlockSpec(memory_space=pltpu.VMEM)
    lanes = (streams, rows, width)
    return pl.pallas_call(
        functools.partial(moe_kernel, chips),
        out_shape=jax.ShapeDtypeStruct(state.shape, jnp.bfloat16),
        in_specs=[hbm] * 3 + [vmem] * 5,
        out_specs=hbm,
        scratch_shapes=[
            pltpu.VMEM(lanes, jnp.bfloat16),
            pltpu.VMEM(lanes, jnp.bfloat16),
            pltpu.VMEM(lanes, jnp.bfloat16),
            pltpu.VMEM(lanes, jnp.bfloat16),
            pltpu.VMEM(state.shape, jnp.bfloat16),
            pltpu.VMEM((2,) + gate_half.shape, jnp.bfloat16),
            pltpu.VMEM((2,) + up_half.shape, jnp.bfloat16),
            pltpu.VMEM((2,) + down_half.shape, jnp.bfloat16),
            pltpu.SemaphoreType.DMA((streams, chips)),
            pltpu.SemaphoreType.DMA((streams, chips)),
            pltpu.SemaphoreType.DMA((streams, chips)),
            pltpu.SemaphoreType.DMA((streams, chips)),
            pltpu.SemaphoreType.DMA((2, streams)),
            pltpu.SemaphoreType.DMA((3, 3)),
            pltpu.SemaphoreType.DMA((2, streams)),
        ],
        compiler_params=pltpu.CompilerParams(
            collective_id=0, has_side_effects=True, vmem_limit_bytes=62 * 1024 * 1024
        ),
    )(gate_half, up_half, down_half, state, gain, pick, comb_hi, comb_lo)


def body(streams, norm_gain, w_gate, w_up, w_down, routes, gate_weights):
    experts = lax.axis_size("ez")
    _, stream_count, tok_rows, top_count = routes.shape
    capacity = 2 * tok_rows * top_count // experts
    lane_count = experts * capacity
    pairs = tok_rows * top_count
    chosen = routes[0].reshape(stream_count, pairs)
    earlier = jnp.arange(pairs)[None, :] < jnp.arange(pairs)[:, None]
    same = (chosen[:, :, None] == chosen[:, None, :]) & earlier[None]
    slot_rank = jnp.sum(same.astype(jnp.int32), axis=-1)
    lane_of = (chosen * capacity + slot_rank).reshape(stream_count, tok_rows, top_count)
    matches = lane_of[..., None] == jnp.arange(lane_count, dtype=jnp.int32)
    pick = jnp.any(matches, axis=2).astype(jnp.bfloat16).transpose(0, 2, 1)
    combine = jnp.sum(jnp.where(matches, gate_weights[0][..., None], 0.0), axis=2)
    comb_hi = combine.astype(jnp.bfloat16)
    comb_lo = (combine - comb_hi.astype(jnp.float32)).astype(jnp.bfloat16)
    relayed = expert_pass(
        pick, w_gate[0, 0], w_up[0, 0], w_down[0, 0],
        streams[0], norm_gain, comb_hi, comb_lo,
    )
    return relayed[None]


def solution(mesh):
    pipe_size, expert_size = mesh.devices.shape
    split = Mesh(
        np.asarray(mesh.devices).reshape(pipe_size, expert_size // 2, 2), ("pipe", "ez", "ec")
    )
    tok = ("ez", "ec")
    return jax.shard_map(
        body,
        mesh=split,
        in_specs=(
            P("pipe", None, tok, None),
            P("pipe", None),
            P("pipe", tok, None, None),
            P("pipe", tok, None, None),
            P("pipe", tok, None, None),
            P("pipe", None, tok, None),
            P("pipe", None, tok, None),
        ),
        out_specs=P("pipe", None, tok, None),
        check_vma=False,
    )
```

```python
import functools

import jax
import jax.numpy as jnp
import numpy as np
from jax import lax
from jax.experimental import pallas as pl
from jax.experimental.pallas import tpu as pltpu
from jax.sharding import Mesh
from jax.sharding import PartitionSpec as P


def from_behind(value, axis, steps):
    count = lax.axis_size(axis)
    pairs = [(source, (source + steps) % count) for source in range(count)]
    return lax.ppermute(value, axis, pairs)


MESH = pl.DeviceIdType.MESH


def moe_kernel(
    chips, wg_hbm, wu_hbm, wd_hbm, state_ref, gain_ref, pick_ref, hi_ref, lo_ref, next_hbm,
    xs, recv, res, ys, mixed, wg, wu, wd, dsend, drecv, rsend, rrecv, lsem, wsem, psem,
):
    streams, rows, width = recv.shape
    cap = rows // chips
    pipe = lax.axis_index("pipe")
    pipes = lax.axis_size("pipe")
    me = lax.axis_index("ez")
    core = lax.axis_index("ec")

    def dev(p):
        return (pipe, p, core)

    def blk(p):
        return pl.ds(pl.multiple_of(p * cap, cap), cap)

    sibling = (pipe, me, 1 - core)
    weights = ((wg_hbm, wg), (wu_hbm, wu), (wd_hbm, wd))
    own_copies = [
        pltpu.make_async_copy(src, dst.at[core], wsem.at[0, i])
        for i, (src, dst) in enumerate(weights)
    ]
    barrier = pltpu.get_barrier_semaphore()
    for k in range(1, chips):
        pl.semaphore_signal(
            barrier, inc=1, device_id=dev(lax.rem(me + k, chips)), device_id_type=MESH
        )
    pl.semaphore_signal(barrier, inc=1, device_id=sibling, device_id_type=MESH)
    section = (lax.rem(pipe + 1, pipes), lax.rem(pipe + pipes - 1, pipes))
    for p in section:
        pl.semaphore_signal(barrier, inc=1, device_id=(p, me, core), device_id_type=MESH)
    pl.semaphore_wait(barrier, chips + 2)

    to_sibling = [
        pltpu.make_async_remote_copy(
            src_ref=src, dst_ref=dst.at[core], send_sem=wsem.at[1, i], recv_sem=wsem.at[2, i],
            device_id=sibling, device_id_type=MESH,
        )
        for i, (src, dst) in enumerate(weights)
    ]
    from_sibling = [
        pltpu.make_async_remote_copy(
            src_ref=src, dst_ref=dst.at[1 - core], send_sem=wsem.at[1, i],
            recv_sem=wsem.at[2, i], device_id=sibling, device_id_type=MESH,
        )
        for i, (src, dst) in enumerate(weights)
    ]

    def dispatch(s, k):
        p = lax.rem(me + k, chips)
        return pltpu.make_async_remote_copy(
            src_ref=xs.at[s, blk(p)], dst_ref=recv.at[s, blk(me)],
            send_sem=dsend.at[s, k], recv_sem=drecv.at[s, me],
            device_id=dev(p), device_id_type=MESH,
        )

    def dispatch_in(s, k):
        q = lax.rem(me + chips - k, chips)
        return pltpu.make_async_remote_copy(
            src_ref=xs.at[s, blk(q)], dst_ref=recv.at[s, blk(q)],
            send_sem=dsend.at[s, k], recv_sem=drecv.at[s, q],
            device_id=dev(q), device_id_type=MESH,
        )

    def back(s, k):
        p = lax.rem(me + k, chips)
        return pltpu.make_async_remote_copy(
            src_ref=res.at[s, blk(p)], dst_ref=ys.at[s, blk(me)],
            send_sem=rsend.at[s, k], recv_sem=rrecv.at[s, me],
            device_id=dev(p), device_id_type=MESH,
        )

    def back_in(s, k):
        q = lax.rem(me + chips - k, chips)
        return pltpu.make_async_remote_copy(
            src_ref=res.at[s, blk(q)], dst_ref=ys.at[s, blk(q)],
            send_sem=rsend.at[s, k], recv_sem=rrecv.at[s, q],
            device_id=dev(q), device_id_type=MESH,
        )

    local_in = [
        pltpu.make_async_copy(xs.at[s, blk(me)], recv.at[s, blk(me)], lsem.at[0, s])
        for s in range(streams)
    ]
    local_out = [
        pltpu.make_async_copy(res.at[s, blk(me)], ys.at[s, blk(me)], lsem.at[1, s])
        for s in range(streams)
    ]
    for s in range(streams):
        state = state_ref[s].astype(jnp.float32)
        scale = lax.rsqrt(jnp.mean(state * state, axis=-1, keepdims=True) + 1e-06)
        normed = (state * scale * gain_ref[...]).astype(jnp.bfloat16)
        xs[s] = jnp.dot(pick_ref[s], normed, preferred_element_type=jnp.float32).astype(
            jnp.bfloat16
        )
        local_in[s].start()
        for k in range(1, chips):
            dispatch(s, k).start()
    for c in own_copies:
        c.start()
    for c in to_sibling:
        c.start()
    for c in own_copies:
        c.wait()
    for c in from_sibling:
        c.wait_recv()
    for c in to_sibling:
        c.wait_send()

    tile = 128
    for s in range(streams):
        local_in[s].wait()
        for k in range(1, chips):
            dispatch_in(s, k).wait_recv()
        for b in range(rows // tile):
            x = recv[s, pl.ds(b * tile, tile), :]
            total = None
            for j in range(2):
                gate_val = jnp.dot(x, wg[j], preferred_element_type=jnp.float32)
                up_val = jnp.dot(x, wu[j], preferred_element_type=jnp.float32)
                hidden = (jax.nn.silu(gate_val) * up_val).astype(jnp.bfloat16)
                part = jnp.dot(hidden, wd[j], preferred_element_type=jnp.float32)
                part = part.astype(jnp.bfloat16).astype(jnp.float32)
                total = part if total is None else total + part
            res[s, pl.ds(b * tile, tile), :] = total.astype(jnp.bfloat16)
        local_out[s].start()
        for k in range(1, chips):
            back(s, k).start()

    for s in range(streams):
        for k in range(1, chips):
            dispatch(s, k).wait_send()
    relay = []
    for s in range(streams):
        local_out[s].wait()
        for k in range(1, chips):
            back_in(s, k).wait_recv()
        rows_back = ys[s]
        total = state_ref[s].astype(jnp.float32)
        total = total + jnp.dot(hi_ref[s], rows_back, preferred_element_type=jnp.float32)
        total = total + jnp.dot(lo_ref[s], rows_back, preferred_element_type=jnp.float32)
        mixed[s] = total.astype(jnp.bfloat16)
        send = pltpu.make_async_remote_copy(
            src_ref=mixed.at[s], dst_ref=next_hbm.at[s], send_sem=psem.at[0, s],
            recv_sem=psem.at[1, s], device_id=(section[s], me, core), device_id_type=MESH,
        )
        send.start()
        relay.append(send)
    for s in range(streams):
        for k in range(1, chips):
            back(s, k).wait_send()
    for send in relay:
        send.wait()


def expert_pass(pick, gate_half, up_half, down_half, state, gain, comb_hi, comb_lo):
    streams, rows, _ = pick.shape
    width = state.shape[-1]
    chips = lax.axis_size("ez")
    hbm = pl.BlockSpec(memory_space=pl.ANY)
    vmem = pl.BlockSpec(memory_space=pltpu.VMEM)
    lanes = (streams, rows, width)
    return pl.pallas_call(
        functools.partial(moe_kernel, chips),
        out_shape=jax.ShapeDtypeStruct(state.shape, jnp.bfloat16),
        in_specs=[hbm] * 3 + [vmem] * 5,
        out_specs=hbm,
        scratch_shapes=[
            pltpu.VMEM(lanes, jnp.bfloat16),
            pltpu.VMEM(lanes, jnp.bfloat16),
            pltpu.VMEM(lanes, jnp.bfloat16),
            pltpu.VMEM(lanes, jnp.bfloat16),
            pltpu.VMEM(state.shape, jnp.bfloat16),
            pltpu.VMEM((2,) + gate_half.shape, jnp.bfloat16),
            pltpu.VMEM((2,) + up_half.shape, jnp.bfloat16),
            pltpu.VMEM((2,) + down_half.shape, jnp.bfloat16),
            pltpu.SemaphoreType.DMA((streams, chips)),
            pltpu.SemaphoreType.DMA((streams, chips)),
            pltpu.SemaphoreType.DMA((streams, chips)),
            pltpu.SemaphoreType.DMA((streams, chips)),
            pltpu.SemaphoreType.DMA((2, streams)),
            pltpu.SemaphoreType.DMA((3, 3)),
            pltpu.SemaphoreType.DMA((2, streams)),
        ],
        compiler_params=pltpu.CompilerParams(
            collective_id=0, has_side_effects=True, vmem_limit_bytes=62 * 1024 * 1024
        ),
    )(gate_half, up_half, down_half, state, gain, pick, comb_hi, comb_lo)


def body(streams, norm_gain, w_gate, w_up, w_down, routes, gate_weights):
    experts = lax.axis_size("ez")
    _, stream_count, tok_rows, top_count = routes.shape
    capacity = 2 * tok_rows * top_count // experts
    lane_count = experts * capacity
    pairs = tok_rows * top_count
    chosen = routes[0].reshape(stream_count, pairs)
    earlier = jnp.arange(pairs)[None, :] < jnp.arange(pairs)[:, None]
    same = (chosen[:, :, None] == chosen[:, None, :]) & earlier[None]
    slot_rank = jnp.sum(same.astype(jnp.int32), axis=-1)
    lane_of = (chosen * capacity + slot_rank).reshape(stream_count, tok_rows, top_count)
    matches = lane_of[..., None] == jnp.arange(lane_count, dtype=jnp.int32)
    pick = jnp.any(matches, axis=2).astype(jnp.bfloat16).transpose(0, 2, 1)
    combine = jnp.sum(jnp.where(matches, gate_weights[0][..., None], 0.0), axis=2)
    comb_hi = combine.astype(jnp.bfloat16)
    comb_lo = (combine - comb_hi.astype(jnp.float32)).astype(jnp.bfloat16)
    relayed = expert_pass(
        pick, w_gate[0, 0], w_up[0, 0], w_down[0, 0],
        streams[0], norm_gain, comb_hi, comb_lo,
    )
    return relayed[None]


def solution(mesh):
    pipe_size, expert_size = mesh.devices.shape
    split = Mesh(
        np.asarray(mesh.devices).reshape(pipe_size, expert_size // 2, 2), ("pipe", "ez", "ec")
    )
    tok = ("ez", "ec")
    return jax.shard_map(
        body,
        mesh=split,
        in_specs=(
            P("pipe", None, tok, None),
            P("pipe", None),
            P("pipe", tok, None, None),
            P("pipe", tok, None, None),
            P("pipe", tok, None, None),
            P("pipe", None, tok, None),
            P("pipe", None, tok, None),
        ),
        out_specs=P("pipe", None, tok, None),
        check_vma=False,
    )
```

```python
import functools

import jax
import jax.numpy as jnp
import numpy as np
from jax import lax
from jax.experimental import pallas as pl
from jax.experimental.pallas import tpu as pltpu
from jax.sharding import Mesh
from jax.sharding import PartitionSpec as P


def from_behind(value, axis, steps):
    count = lax.axis_size(axis)
    pairs = [(source, (source + steps) % count) for source in range(count)]
    return lax.ppermute(value, axis, pairs)


MESH = pl.DeviceIdType.MESH


def moe_kernel(
    chips, wg_hbm, wu_hbm, wd_hbm, state_ref, gain_ref, pick_ref, hi_ref, lo_ref, next_hbm,
    xs, recv, res, ys, mixed, wg, wu, wd, dsend, drecv, rsend, rrecv, lsem, wsem, psem,
):
    streams, rows, width = recv.shape
    cap = rows // chips
    pipe = lax.axis_index("pipe")
    pipes = lax.axis_size("pipe")
    me = lax.axis_index("ez")
    core = lax.axis_index("ec")

    def dev(p):
        return (pipe, p, core)

    def blk(p):
        return pl.ds(pl.multiple_of(p * cap, cap), cap)

    sibling = (pipe, me, 1 - core)
    weights = ((wg_hbm, wg), (wu_hbm, wu), (wd_hbm, wd))
    own_copies = [
        pltpu.make_async_copy(src, dst.at[core], wsem.at[0, i])
        for i, (src, dst) in enumerate(weights)
    ]
    for c in own_copies:
        c.start()

    def select_rows(s):
        state = state_ref[s].astype(jnp.float32)
        scale = lax.rsqrt(jnp.mean(state * state, axis=-1, keepdims=True) + 1e-06)
        normed = (state * scale * gain_ref[...]).astype(jnp.bfloat16)
        xs[s] = jnp.dot(pick_ref[s], normed, preferred_element_type=jnp.float32).astype(
            jnp.bfloat16
        )

    select_rows(0)
    barrier = pltpu.get_barrier_semaphore()
    for k in range(1, chips):
        pl.semaphore_signal(
            barrier, inc=1, device_id=dev(lax.rem(me + k, chips)), device_id_type=MESH
        )
    pl.semaphore_signal(barrier, inc=1, device_id=sibling, device_id_type=MESH)
    section = (lax.rem(pipe + 1, pipes), lax.rem(pipe + pipes - 1, pipes))
    for p in section:
        pl.semaphore_signal(barrier, inc=1, device_id=(p, me, core), device_id_type=MESH)
    pl.semaphore_wait(barrier, chips + 2)

    to_sibling = [
        pltpu.make_async_remote_copy(
            src_ref=src, dst_ref=dst.at[core], send_sem=wsem.at[1, i], recv_sem=wsem.at[2, i],
            device_id=sibling, device_id_type=MESH,
        )
        for i, (src, dst) in enumerate(weights)
    ]
    from_sibling = [
        pltpu.make_async_remote_copy(
            src_ref=src, dst_ref=dst.at[1 - core], send_sem=wsem.at[1, i],
            recv_sem=wsem.at[2, i], device_id=sibling, device_id_type=MESH,
        )
        for i, (src, dst) in enumerate(weights)
    ]

    def dispatch(s, k):
        p = lax.rem(me + k, chips)
        return pltpu.make_async_remote_copy(
            src_ref=xs.at[s, blk(p)], dst_ref=recv.at[s, blk(me)],
            send_sem=dsend.at[s, k], recv_sem=drecv.at[s, me],
            device_id=dev(p), device_id_type=MESH,
        )

    def dispatch_in(s, k):
        q = lax.rem(me + chips - k, chips)
        return pltpu.make_async_remote_copy(
            src_ref=xs.at[s, blk(q)], dst_ref=recv.at[s, blk(q)],
            send_sem=dsend.at[s, k], recv_sem=drecv.at[s, q],
            device_id=dev(q), device_id_type=MESH,
        )

    def back(s, k):
        p = lax.rem(me + k, chips)
        return pltpu.make_async_remote_copy(
            src_ref=res.at[s, blk(p)], dst_ref=ys.at[s, blk(me)],
            send_sem=rsend.at[s, k], recv_sem=rrecv.at[s, me],
            device_id=dev(p), device_id_type=MESH,
        )

    def back_in(s, k):
        q = lax.rem(me + chips - k, chips)
        return pltpu.make_async_remote_copy(
            src_ref=res.at[s, blk(q)], dst_ref=ys.at[s, blk(q)],
            send_sem=rsend.at[s, k], recv_sem=rrecv.at[s, q],
            device_id=dev(q), device_id_type=MESH,
        )

    local_in = [
        pltpu.make_async_copy(xs.at[s, blk(me)], recv.at[s, blk(me)], lsem.at[0, s])
        for s in range(streams)
    ]
    local_out = [
        pltpu.make_async_copy(res.at[s, blk(me)], ys.at[s, blk(me)], lsem.at[1, s])
        for s in range(streams)
    ]
    for s in range(streams):
        if s > 0:
            select_rows(s)
        local_in[s].start()
        for k in range(1, chips):
            dispatch(s, k).start()
    for c in to_sibling:
        c.start()
    for c in own_copies:
        c.wait()
    for c in from_sibling:
        c.wait_recv()
    for c in to_sibling:
        c.wait_send()

    tile = 128
    for s in range(streams):
        local_in[s].wait()
        for k in range(1, chips):
            dispatch_in(s, k).wait_recv()
        for b in range(rows // tile):
            x = recv[s, pl.ds(b * tile, tile), :]
            total = None
            for j in range(2):
                gate_val = jnp.dot(x, wg[j], preferred_element_type=jnp.float32)
                up_val = jnp.dot(x, wu[j], preferred_element_type=jnp.float32)
                hidden = (jax.nn.silu(gate_val) * up_val).astype(jnp.bfloat16)
                part = jnp.dot(hidden, wd[j], preferred_element_type=jnp.float32)
                part = part.astype(jnp.bfloat16).astype(jnp.float32)
                total = part if total is None else total + part
            res[s, pl.ds(b * tile, tile), :] = total.astype(jnp.bfloat16)
        local_out[s].start()
        for k in range(1, chips):
            back(s, k).start()

    for s in range(streams):
        for k in range(1, chips):
            dispatch(s, k).wait_send()
    relay = []
    for s in range(streams):
        local_out[s].wait()
        for k in range(1, chips):
            back_in(s, k).wait_recv()
        rows_back = ys[s]
        total = state_ref[s].astype(jnp.float32)
        total = total + jnp.dot(hi_ref[s], rows_back, preferred_element_type=jnp.float32)
        total = total + jnp.dot(lo_ref[s], rows_back, preferred_element_type=jnp.float32)
        mixed[s] = total.astype(jnp.bfloat16)
        send = pltpu.make_async_remote_copy(
            src_ref=mixed.at[s], dst_ref=next_hbm.at[s], send_sem=psem.at[0, s],
            recv_sem=psem.at[1, s], device_id=(section[s], me, core), device_id_type=MESH,
        )
        send.start()
        relay.append(send)
    for s in range(streams):
        for k in range(1, chips):
            back(s, k).wait_send()
    for send in relay:
        send.wait()


def expert_pass(pick, gate_half, up_half, down_half, state, gain, comb_hi, comb_lo):
    streams, rows, _ = pick.shape
    width = state.shape[-1]
    chips = lax.axis_size("ez")
    hbm = pl.BlockSpec(memory_space=pl.ANY)
    vmem = pl.BlockSpec(memory_space=pltpu.VMEM)
    lanes = (streams, rows, width)
    return pl.pallas_call(
        functools.partial(moe_kernel, chips),
        out_shape=jax.ShapeDtypeStruct(state.shape, jnp.bfloat16),
        in_specs=[hbm] * 3 + [vmem] * 5,
        out_specs=hbm,
        scratch_shapes=[
            pltpu.VMEM(lanes, jnp.bfloat16),
            pltpu.VMEM(lanes, jnp.bfloat16),
            pltpu.VMEM(lanes, jnp.bfloat16),
            pltpu.VMEM(lanes, jnp.bfloat16),
            pltpu.VMEM(state.shape, jnp.bfloat16),
            pltpu.VMEM((2,) + gate_half.shape, jnp.bfloat16),
            pltpu.VMEM((2,) + up_half.shape, jnp.bfloat16),
            pltpu.VMEM((2,) + down_half.shape, jnp.bfloat16),
            pltpu.SemaphoreType.DMA((streams, chips)),
            pltpu.SemaphoreType.DMA((streams, chips)),
            pltpu.SemaphoreType.DMA((streams, chips)),
            pltpu.SemaphoreType.DMA((streams, chips)),
            pltpu.SemaphoreType.DMA((2, streams)),
            pltpu.SemaphoreType.DMA((3, 3)),
            pltpu.SemaphoreType.DMA((2, streams)),
        ],
        compiler_params=pltpu.CompilerParams(
            collective_id=0, has_side_effects=True, vmem_limit_bytes=62 * 1024 * 1024
        ),
    )(gate_half, up_half, down_half, state, gain, pick, comb_hi, comb_lo)


def body(streams, norm_gain, w_gate, w_up, w_down, routes, gate_weights):
    experts = lax.axis_size("ez")
    _, stream_count, tok_rows, top_count = routes.shape
    capacity = 2 * tok_rows * top_count // experts
    lane_count = experts * capacity
    pairs = tok_rows * top_count
    chosen = routes[0].reshape(stream_count, pairs)
    earlier = jnp.arange(pairs)[None, :] < jnp.arange(pairs)[:, None]
    same = (chosen[:, :, None] == chosen[:, None, :]) & earlier[None]
    slot_rank = jnp.sum(same.astype(jnp.int32), axis=-1)
    lane_of = (chosen * capacity + slot_rank).reshape(stream_count, tok_rows, top_count)
    matches = lane_of[..., None] == jnp.arange(lane_count, dtype=jnp.int32)
    pick = jnp.any(matches, axis=2).astype(jnp.bfloat16).transpose(0, 2, 1)
    combine = jnp.sum(jnp.where(matches, gate_weights[0][..., None], 0.0), axis=2)
    comb_hi = combine.astype(jnp.bfloat16)
    comb_lo = (combine - comb_hi.astype(jnp.float32)).astype(jnp.bfloat16)
    relayed = expert_pass(
        pick, w_gate[0, 0], w_up[0, 0], w_down[0, 0],
        streams[0], norm_gain, comb_hi, comb_lo,
    )
    return relayed[None]


def solution(mesh):
    pipe_size, expert_size = mesh.devices.shape
    split = Mesh(
        np.asarray(mesh.devices).reshape(pipe_size, expert_size // 2, 2), ("pipe", "ez", "ec")
    )
    tok = ("ez", "ec")
    return jax.shard_map(
        body,
        mesh=split,
        in_specs=(
            P("pipe", None, tok, None),
            P("pipe", None),
            P("pipe", tok, None, None),
            P("pipe", tok, None, None),
            P("pipe", tok, None, None),
            P("pipe", None, tok, None),
            P("pipe", None, tok, None),
        ),
        out_specs=P("pipe", None, tok, None),
        check_vma=False,
    )
```

```python
import functools

import jax
import jax.numpy as jnp
import numpy as np
from jax import lax
from jax.experimental import pallas as pl
from jax.experimental.pallas import tpu as pltpu
from jax.sharding import Mesh
from jax.sharding import PartitionSpec as P


def from_behind(value, axis, steps):
    count = lax.axis_size(axis)
    pairs = [(source, (source + steps) % count) for source in range(count)]
    return lax.ppermute(value, axis, pairs)


MESH = pl.DeviceIdType.MESH


def moe_kernel(
    chips, wg_hbm, wu_hbm, wd_hbm, state_ref, gain_ref, pick_ref, hi_ref, lo_ref, next_hbm,
    xs, recv, res, ys, mixed, wg, wu, wd, dsend, drecv, rsend, rrecv, lsem, wsem, psem,
):
    streams, rows, width = recv.shape
    cap = rows // chips
    pipe = lax.axis_index("pipe")
    pipes = lax.axis_size("pipe")
    me = lax.axis_index("ez")
    core = lax.axis_index("ec")

    def dev(p):
        return (pipe, p, core)

    def blk(p):
        return pl.ds(pl.multiple_of(p * cap, cap), cap)

    sibling = (pipe, me, 1 - core)
    weights = ((wg_hbm, wg), (wu_hbm, wu), (wd_hbm, wd))
    own_copies = [
        pltpu.make_async_copy(src, dst.at[core], wsem.at[0, i])
        for i, (src, dst) in enumerate(weights)
    ]
    for c in own_copies:
        c.start()

    barrier = pltpu.get_barrier_semaphore()
    for k in range(1, chips):
        pl.semaphore_signal(
            barrier, inc=1, device_id=dev(lax.rem(me + k, chips)), device_id_type=MESH
        )
    pl.semaphore_signal(barrier, inc=1, device_id=sibling, device_id_type=MESH)
    section = (lax.rem(pipe + 1, pipes), lax.rem(pipe + pipes - 1, pipes))
    for p in section:
        pl.semaphore_signal(barrier, inc=1, device_id=(p, me, core), device_id_type=MESH)
    pl.semaphore_wait(barrier, chips + 2)

    to_sibling = [
        pltpu.make_async_remote_copy(
            src_ref=src, dst_ref=dst.at[core], send_sem=wsem.at[1, i], recv_sem=wsem.at[2, i],
            device_id=sibling, device_id_type=MESH,
        )
        for i, (src, dst) in enumerate(weights)
    ]
    from_sibling = [
        pltpu.make_async_remote_copy(
            src_ref=src, dst_ref=dst.at[1 - core], send_sem=wsem.at[1, i],
            recv_sem=wsem.at[2, i], device_id=sibling, device_id_type=MESH,
        )
        for i, (src, dst) in enumerate(weights)
    ]

    def dispatch(s, k):
        p = lax.rem(me + k, chips)
        return pltpu.make_async_remote_copy(
            src_ref=xs.at[s, blk(p)], dst_ref=recv.at[s, blk(me)],
            send_sem=dsend.at[s, k], recv_sem=drecv.at[s, me],
            device_id=dev(p), device_id_type=MESH,
        )

    def dispatch_in(s, k):
        q = lax.rem(me + chips - k, chips)
        return pltpu.make_async_remote_copy(
            src_ref=xs.at[s, blk(q)], dst_ref=recv.at[s, blk(q)],
            send_sem=dsend.at[s, k], recv_sem=drecv.at[s, q],
            device_id=dev(q), device_id_type=MESH,
        )

    def back(s, k):
        p = lax.rem(me + k, chips)
        return pltpu.make_async_remote_copy(
            src_ref=res.at[s, blk(p)], dst_ref=ys.at[s, blk(me)],
            send_sem=rsend.at[s, k], recv_sem=rrecv.at[s, me],
            device_id=dev(p), device_id_type=MESH,
        )

    def back_in(s, k):
        q = lax.rem(me + chips - k, chips)
        return pltpu.make_async_remote_copy(
            src_ref=res.at[s, blk(q)], dst_ref=ys.at[s, blk(q)],
            send_sem=rsend.at[s, k], recv_sem=rrecv.at[s, q],
            device_id=dev(q), device_id_type=MESH,
        )

    farthest_first = sorted(range(1, chips), key=lambda k: -min(k, chips - k))
    local_in = [
        pltpu.make_async_copy(xs.at[s, blk(me)], recv.at[s, blk(me)], lsem.at[0, s])
        for s in range(streams)
    ]
    local_out = [
        pltpu.make_async_copy(res.at[s, blk(me)], ys.at[s, blk(me)], lsem.at[1, s])
        for s in range(streams)
    ]
    for s in range(streams):
        state = state_ref[s].astype(jnp.float32)
        scale = lax.rsqrt(jnp.mean(state * state, axis=-1, keepdims=True) + 1e-06)
        normed = (state * scale * gain_ref[...]).astype(jnp.bfloat16)
        xs[s] = jnp.dot(pick_ref[s], normed, preferred_element_type=jnp.float32).astype(
            jnp.bfloat16
        )
        local_in[s].start()
        for k in farthest_first:
            dispatch(s, k).start()
    for c in to_sibling:
        c.start()
    for c in own_copies:
        c.wait()
    for c in from_sibling:
        c.wait_recv()
    for c in to_sibling:
        c.wait_send()

    tile = 128
    for s in range(streams):
        local_in[s].wait()
        for k in range(1, chips):
            dispatch_in(s, k).wait_recv()
        for b in range(rows // tile):
            x = recv[s, pl.ds(b * tile, tile), :]
            total = None
            for j in range(2):
                gate_val = jnp.dot(x, wg[j], preferred_element_type=jnp.float32)
                up_val = jnp.dot(x, wu[j], preferred_element_type=jnp.float32)
                hidden = (jax.nn.silu(gate_val) * up_val).astype(jnp.bfloat16)
                part = jnp.dot(hidden, wd[j], preferred_element_type=jnp.float32)
                part = part.astype(jnp.bfloat16).astype(jnp.float32)
                total = part if total is None else total + part
            res[s, pl.ds(b * tile, tile), :] = total.astype(jnp.bfloat16)
        local_out[s].start()
        for k in farthest_first:
            back(s, k).start()

    for s in range(streams):
        for k in range(1, chips):
            dispatch(s, k).wait_send()
    relay = []
    for s in range(streams):
        local_out[s].wait()
        for k in range(1, chips):
            back_in(s, k).wait_recv()
        rows_back = ys[s]
        total = state_ref[s].astype(jnp.float32)
        total = total + jnp.dot(hi_ref[s], rows_back, preferred_element_type=jnp.float32)
        total = total + jnp.dot(lo_ref[s], rows_back, preferred_element_type=jnp.float32)
        mixed[s] = total.astype(jnp.bfloat16)
        send = pltpu.make_async_remote_copy(
            src_ref=mixed.at[s], dst_ref=next_hbm.at[s], send_sem=psem.at[0, s],
            recv_sem=psem.at[1, s], device_id=(section[s], me, core), device_id_type=MESH,
        )
        send.start()
        relay.append(send)
    for s in range(streams):
        for k in range(1, chips):
            back(s, k).wait_send()
    for send in relay:
        send.wait()


def expert_pass(pick, gate_half, up_half, down_half, state, gain, comb_hi, comb_lo):
    streams, rows, _ = pick.shape
    width = state.shape[-1]
    chips = lax.axis_size("ez")
    hbm = pl.BlockSpec(memory_space=pl.ANY)
    vmem = pl.BlockSpec(memory_space=pltpu.VMEM)
    lanes = (streams, rows, width)
    return pl.pallas_call(
        functools.partial(moe_kernel, chips),
        out_shape=jax.ShapeDtypeStruct(state.shape, jnp.bfloat16),
        in_specs=[hbm] * 3 + [vmem] * 5,
        out_specs=hbm,
        scratch_shapes=[
            pltpu.VMEM(lanes, jnp.bfloat16),
            pltpu.VMEM(lanes, jnp.bfloat16),
            pltpu.VMEM(lanes, jnp.bfloat16),
            pltpu.VMEM(lanes, jnp.bfloat16),
            pltpu.VMEM(state.shape, jnp.bfloat16),
            pltpu.VMEM((2,) + gate_half.shape, jnp.bfloat16),
            pltpu.VMEM((2,) + up_half.shape, jnp.bfloat16),
            pltpu.VMEM((2,) + down_half.shape, jnp.bfloat16),
            pltpu.SemaphoreType.DMA((streams, chips)),
            pltpu.SemaphoreType.DMA((streams, chips)),
            pltpu.SemaphoreType.DMA((streams, chips)),
            pltpu.SemaphoreType.DMA((streams, chips)),
            pltpu.SemaphoreType.DMA((2, streams)),
            pltpu.SemaphoreType.DMA((3, 3)),
            pltpu.SemaphoreType.DMA((2, streams)),
        ],
        compiler_params=pltpu.CompilerParams(
            collective_id=0, has_side_effects=True, vmem_limit_bytes=62 * 1024 * 1024
        ),
    )(gate_half, up_half, down_half, state, gain, pick, comb_hi, comb_lo)


def body(streams, norm_gain, w_gate, w_up, w_down, routes, gate_weights):
    experts = lax.axis_size("ez")
    _, stream_count, tok_rows, top_count = routes.shape
    capacity = 2 * tok_rows * top_count // experts
    lane_count = experts * capacity
    pairs = tok_rows * top_count
    chosen = routes[0].reshape(stream_count, pairs)
    earlier = jnp.arange(pairs)[None, :] < jnp.arange(pairs)[:, None]
    same = (chosen[:, :, None] == chosen[:, None, :]) & earlier[None]
    slot_rank = jnp.sum(same.astype(jnp.int32), axis=-1)
    lane_of = (chosen * capacity + slot_rank).reshape(stream_count, tok_rows, top_count)
    matches = lane_of[..., None] == jnp.arange(lane_count, dtype=jnp.int32)
    pick = jnp.any(matches, axis=2).astype(jnp.bfloat16).transpose(0, 2, 1)
    combine = jnp.sum(jnp.where(matches, gate_weights[0][..., None], 0.0), axis=2)
    comb_hi = combine.astype(jnp.bfloat16)
    comb_lo = (combine - comb_hi.astype(jnp.float32)).astype(jnp.bfloat16)
    relayed = expert_pass(
        pick, w_gate[0, 0], w_up[0, 0], w_down[0, 0],
        streams[0], norm_gain, comb_hi, comb_lo,
    )
    return relayed[None]


def solution(mesh):
    pipe_size, expert_size = mesh.devices.shape
    split = Mesh(
        np.asarray(mesh.devices).reshape(pipe_size, expert_size // 2, 2), ("pipe", "ez", "ec")
    )
    tok = ("ez", "ec")
    return jax.shard_map(
        body,
        mesh=split,
        in_specs=(
            P("pipe", None, tok, None),
            P("pipe", None),
            P("pipe", tok, None, None),
            P("pipe", tok, None, None),
            P("pipe", tok, None, None),
            P("pipe", None, tok, None),
            P("pipe", None, tok, None),
        ),
        out_specs=P("pipe", None, tok, None),
        check_vma=False,
    )
```

```python
import functools

import jax
import jax.numpy as jnp
import numpy as np
from jax import lax
from jax.experimental import pallas as pl
from jax.experimental.pallas import tpu as pltpu
from jax.sharding import Mesh
from jax.sharding import PartitionSpec as P


def from_behind(value, axis, steps):
    count = lax.axis_size(axis)
    pairs = [(source, (source + steps) % count) for source in range(count)]
    return lax.ppermute(value, axis, pairs)


MESH = pl.DeviceIdType.MESH


def moe_kernel(
    chips, wg_hbm, wu_hbm, wd_hbm, state_ref, gain_ref, pick_ref, hi_ref, lo_ref, next_hbm,
    xs, recv, res, ys, mixed, wg, wu, wd, dsend, drecv, rsend, rrecv, lsem, wsem, psem,
):
    streams, rows, width = recv.shape
    cap = rows // chips
    pipe = lax.axis_index("pipe")
    pipes = lax.axis_size("pipe")
    me = lax.axis_index("ez")
    core = lax.axis_index("ec")

    def dev(p):
        return (pipe, p, core)

    def blk(p):
        return pl.ds(pl.multiple_of(p * cap, cap), cap)

    sibling = (pipe, me, 1 - core)
    weights = ((wg_hbm, wg), (wu_hbm, wu), (wd_hbm, wd))
    own_copies = [
        pltpu.make_async_copy(src, dst.at[core], wsem.at[0, i])
        for i, (src, dst) in enumerate(weights)
    ]
    for c in own_copies:
        c.start()

    barrier = pltpu.get_barrier_semaphore()
    for k in range(1, chips):
        pl.semaphore_signal(
            barrier, inc=1, device_id=dev(lax.rem(me + k, chips)), device_id_type=MESH
        )
    pl.semaphore_signal(barrier, inc=1, device_id=sibling, device_id_type=MESH)
    section = (lax.rem(pipe + 1, pipes), lax.rem(pipe + pipes - 1, pipes))
    for p in section:
        pl.semaphore_signal(barrier, inc=1, device_id=(p, me, core), device_id_type=MESH)
    pl.semaphore_wait(barrier, chips + 2)

    to_sibling = [
        pltpu.make_async_remote_copy(
            src_ref=src, dst_ref=dst.at[core], send_sem=wsem.at[1, i], recv_sem=wsem.at[2, i],
            device_id=sibling, device_id_type=MESH,
        )
        for i, (src, dst) in enumerate(weights)
    ]
    from_sibling = [
        pltpu.make_async_remote_copy(
            src_ref=src, dst_ref=dst.at[1 - core], send_sem=wsem.at[1, i],
            recv_sem=wsem.at[2, i], device_id=sibling, device_id_type=MESH,
        )
        for i, (src, dst) in enumerate(weights)
    ]

    def dispatch(s, k):
        p = lax.rem(me + k, chips)
        return pltpu.make_async_remote_copy(
            src_ref=xs.at[s, blk(p)], dst_ref=recv.at[s, blk(me)],
            send_sem=dsend.at[s, k], recv_sem=drecv.at[s, me],
            device_id=dev(p), device_id_type=MESH,
        )

    def dispatch_in(s, k):
        q = lax.rem(me + chips - k, chips)
        return pltpu.make_async_remote_copy(
            src_ref=xs.at[s, blk(q)], dst_ref=recv.at[s, blk(q)],
            send_sem=dsend.at[s, k], recv_sem=drecv.at[s, q],
            device_id=dev(q), device_id_type=MESH,
        )

    def back(s, k):
        p = lax.rem(me + k, chips)
        return pltpu.make_async_remote_copy(
            src_ref=res.at[s, blk(p)], dst_ref=ys.at[s, blk(me)],
            send_sem=rsend.at[s, k], recv_sem=rrecv.at[s, me],
            device_id=dev(p), device_id_type=MESH,
        )

    def back_in(s, k):
        q = lax.rem(me + chips - k, chips)
        return pltpu.make_async_remote_copy(
            src_ref=res.at[s, blk(q)], dst_ref=ys.at[s, blk(q)],
            send_sem=rsend.at[s, k], recv_sem=rrecv.at[s, q],
            device_id=dev(q), device_id_type=MESH,
        )

    local_in = [
        pltpu.make_async_copy(xs.at[s, blk(me)], recv.at[s, blk(me)], lsem.at[0, s])
        for s in range(streams)
    ]
    local_out = [
        pltpu.make_async_copy(res.at[s, blk(me)], ys.at[s, blk(me)], lsem.at[1, s])
        for s in range(streams)
    ]
    for s in range(streams):
        state = state_ref[s].astype(jnp.float32)
        scale = lax.rsqrt(jnp.mean(state * state, axis=-1, keepdims=True) + 1e-06)
        normed = (state * scale * gain_ref[...]).astype(jnp.bfloat16)
        xs[s] = jnp.dot(pick_ref[s], normed, preferred_element_type=jnp.float32).astype(
            jnp.bfloat16
        )
        local_in[s].start()
        for k in range(1, chips):
            dispatch(s, k).start()
    for c in to_sibling:
        c.start()
    for c in own_copies:
        c.wait()
    for c in from_sibling:
        c.wait_recv()
    for c in to_sibling:
        c.wait_send()

    tile = rows
    for s in range(streams):
        local_in[s].wait()
        for k in range(1, chips):
            dispatch_in(s, k).wait_recv()
        for b in range(rows // tile):
            x = recv[s, pl.ds(b * tile, tile), :]
            total = None
            for j in range(2):
                gate_val = jnp.dot(x, wg[j], preferred_element_type=jnp.float32)
                up_val = jnp.dot(x, wu[j], preferred_element_type=jnp.float32)
                hidden = (jax.nn.silu(gate_val) * up_val).astype(jnp.bfloat16)
                part = jnp.dot(hidden, wd[j], preferred_element_type=jnp.float32)
                part = part.astype(jnp.bfloat16).astype(jnp.float32)
                total = part if total is None else total + part
            res[s, pl.ds(b * tile, tile), :] = total.astype(jnp.bfloat16)
        local_out[s].start()
        for k in range(1, chips):
            back(s, k).start()

    for s in range(streams):
        for k in range(1, chips):
            dispatch(s, k).wait_send()
    relay = []
    for s in range(streams):
        local_out[s].wait()
        for k in range(1, chips):
            back_in(s, k).wait_recv()
        rows_back = ys[s]
        total = state_ref[s].astype(jnp.float32)
        total = total + jnp.dot(hi_ref[s], rows_back, preferred_element_type=jnp.float32)
        total = total + jnp.dot(lo_ref[s], rows_back, preferred_element_type=jnp.float32)
        mixed[s] = total.astype(jnp.bfloat16)
        send = pltpu.make_async_remote_copy(
            src_ref=mixed.at[s], dst_ref=next_hbm.at[s], send_sem=psem.at[0, s],
            recv_sem=psem.at[1, s], device_id=(section[s], me, core), device_id_type=MESH,
        )
        send.start()
        relay.append(send)
    for s in range(streams):
        for k in range(1, chips):
            back(s, k).wait_send()
    for send in relay:
        send.wait()


def expert_pass(pick, gate_half, up_half, down_half, state, gain, comb_hi, comb_lo):
    streams, rows, _ = pick.shape
    width = state.shape[-1]
    chips = lax.axis_size("ez")
    hbm = pl.BlockSpec(memory_space=pl.ANY)
    vmem = pl.BlockSpec(memory_space=pltpu.VMEM)
    lanes = (streams, rows, width)
    return pl.pallas_call(
        functools.partial(moe_kernel, chips),
        out_shape=jax.ShapeDtypeStruct(state.shape, jnp.bfloat16),
        in_specs=[hbm] * 3 + [vmem] * 5,
        out_specs=hbm,
        scratch_shapes=[
            pltpu.VMEM(lanes, jnp.bfloat16),
            pltpu.VMEM(lanes, jnp.bfloat16),
            pltpu.VMEM(lanes, jnp.bfloat16),
            pltpu.VMEM(lanes, jnp.bfloat16),
            pltpu.VMEM(state.shape, jnp.bfloat16),
            pltpu.VMEM((2,) + gate_half.shape, jnp.bfloat16),
            pltpu.VMEM((2,) + up_half.shape, jnp.bfloat16),
            pltpu.VMEM((2,) + down_half.shape, jnp.bfloat16),
            pltpu.SemaphoreType.DMA((streams, chips)),
            pltpu.SemaphoreType.DMA((streams, chips)),
            pltpu.SemaphoreType.DMA((streams, chips)),
            pltpu.SemaphoreType.DMA((streams, chips)),
            pltpu.SemaphoreType.DMA((2, streams)),
            pltpu.SemaphoreType.DMA((3, 3)),
            pltpu.SemaphoreType.DMA((2, streams)),
        ],
        compiler_params=pltpu.CompilerParams(
            collective_id=0, has_side_effects=True, vmem_limit_bytes=62 * 1024 * 1024
        ),
    )(gate_half, up_half, down_half, state, gain, pick, comb_hi, comb_lo)


def body(streams, norm_gain, w_gate, w_up, w_down, routes, gate_weights):
    experts = lax.axis_size("ez")
    _, stream_count, tok_rows, top_count = routes.shape
    capacity = 2 * tok_rows * top_count // experts
    lane_count = experts * capacity
    pairs = tok_rows * top_count
    chosen = routes[0].reshape(stream_count, pairs)
    earlier = jnp.arange(pairs)[None, :] < jnp.arange(pairs)[:, None]
    same = (chosen[:, :, None] == chosen[:, None, :]) & earlier[None]
    slot_rank = jnp.sum(same.astype(jnp.int32), axis=-1)
    lane_of = (chosen * capacity + slot_rank).reshape(stream_count, tok_rows, top_count)
    matches = lane_of[..., None] == jnp.arange(lane_count, dtype=jnp.int32)
    pick = jnp.any(matches, axis=2).astype(jnp.bfloat16).transpose(0, 2, 1)
    combine = jnp.sum(jnp.where(matches, gate_weights[0][..., None], 0.0), axis=2)
    comb_hi = combine.astype(jnp.bfloat16)
    comb_lo = (combine - comb_hi.astype(jnp.float32)).astype(jnp.bfloat16)
    relayed = expert_pass(
        pick, w_gate[0, 0], w_up[0, 0], w_down[0, 0],
        streams[0], norm_gain, comb_hi, comb_lo,
    )
    return relayed[None]


def solution(mesh):
    pipe_size, expert_size = mesh.devices.shape
    split = Mesh(
        np.asarray(mesh.devices).reshape(pipe_size, expert_size // 2, 2), ("pipe", "ez", "ec")
    )
    tok = ("ez", "ec")
    return jax.shard_map(
        body,
        mesh=split,
        in_specs=(
            P("pipe", None, tok, None),
            P("pipe", None),
            P("pipe", tok, None, None),
            P("pipe", tok, None, None),
            P("pipe", tok, None, None),
            P("pipe", None, tok, None),
            P("pipe", None, tok, None),
        ),
        out_specs=P("pipe", None, tok, None),
        check_vma=False,
    )
```
